32 devices in a mesh: group: 2 (over y), sec: 8 (over z, x), head: 2 (over core).
Axes of the slice: x: 2, y: 2, z: 4, core: 2. Of those that a mesh axis runs over, the one named last changes fastest.
Arguments:
- queries: bfloat16 [64, 8192], P(('group', 'sec'), 'head'), parts along dimension 0, may hold values from -10 to 10
- key_cache: bfloat16 [64, 512, 4, 128], P(('group', 'sec'), None, 'head'), parts along dimension 0, may hold values from -10 to 10
- value_cache: bfloat16 [64, 512, 4, 128], P(('group', 'sec'), None, 'head'), parts along dimension 0, may hold values from -6 to 6
- new_keys: bfloat16 [64, 512], P(('group', 'sec'), 'head'), parts along dimension 0, may hold values from -10 to 10
- new_values: bfloat16 [64, 512], P(('group', 'sec'), 'head'), parts along dimension 0, may hold values from -6 to 6
- history: int32 [64], P(('group', 'sec')), parts along dimension 0, may hold values from 1 to 512, 8192 in all
- tokens: bfloat16 [256, 2048], P(('group', 'sec', 'head')), parts along dimension 0, may hold values from -6 to 6
- expert_ids: int32 [256, 8], P(('group', 'sec', 'head')), parts along dimension 0, may hold values from 0 to 63, all different within a row; in each aligned block of 8 rows (0 to 7, 8 to 15, ...) at most 2 rows name the same one
- gate_values: float32 [256, 8], P(('group', 'sec', 'head')), parts along dimension 0, may hold values from 0.1 to 0.6
- w_gate: bfloat16 [128, 384, 2048], P('sec', 'head'), may hold values from -0.125 to 0.125
- w_up: bfloat16 [128, 384, 2048], P('sec', 'head'), may hold values from -0.125 to 0.125
- w_down: bfloat16 [128, 384, 2048], P('sec', 'head'), may hold values from -0.21875 to 0.21875
Outputs:
- attn_context: bfloat16 [64, 8192], P(('group', 'sec'), 'head'), parts along dimension 0
- expert_output: bfloat16 [256, 2048], P(('group', 'sec', 'head')), parts along dimension 0
The draws below stay inside these ranges and needn't reach their ends.
There are 2 independent parts, one for each index of `group`. The reference program is written for one: setup_inputs(seed, part) draws one part's arguments, and reference() takes and returns one part's arrays. A program takes and returns all parts, laid end to end along the dimension named above; an argument that names none is the same for every part. Nothing has to cross between parts.
Inputs may be any that keep to these rules, and one draw needn't show every extreme that they name: `history`: the lengths of one part sum to 8192, and one of them is 512 in every draw. `expert_ids`: each row names 8 different experts. Among the 8 rows of one device no expert is named by more than 2 rows, and in every draw some expert is named by exactly 2 rows of some device.
All inputs are finite; a program needn't handle non-finite values. No bound on the sum of `history` on one device may be relied on, other than what follows from the above.
Results may differ from the reference program's by a relative error of at most 0.0066.
Values may be sent and summed in bfloat16 or wider, within the bound.
A program may use at most 128 MiB of HBM per device.

```python
import math
import jax
import jax.numpy as jnp
import numpy as np
from jax import lax

D = 2048
FF = 768
EXPERTS = 64
TOP = 8
HQ = 64
KVH = 4
HD = 128
L = 512
TOK_DEV = 8
CAP = 2
REQS = 32
TOKENS = 128
N_SEC = 8
N_HEAD = 2


def draw_queries(key, part):
    drawn = jnp.clip(jax.random.normal(jax.random.fold_in(key, 11), (REQS, HQ * HD), jnp.float32), -6.0, 6.0)
    return drawn.astype(jnp.bfloat16)


def draw_key_cache(key, part):
    drawn = jnp.clip(jax.random.normal(jax.random.fold_in(key, 21), (REQS, L, KVH, HD), jnp.float32), -6.0, 6.0)
    return drawn.astype(jnp.bfloat16)


def draw_new_keys(key, part):
    drawn = jnp.clip(jax.random.normal(jax.random.fold_in(key, 31), (REQS, KVH * HD), jnp.float32), -6.0, 6.0)
    return drawn.astype(jnp.bfloat16)


def block_levels(rng, extent, shards, smallest, top_value):
    gain, own = 1.0, jax.random.fold_in(rng, 6)
    for axis_at, blocks in shards:
        heights = jnp.exp(jax.random.uniform(jax.random.fold_in(own, axis_at), (blocks,), jnp.float32, smallest / len(shards), top_value / len(shards)))
        gain = gain * jnp.repeat(heights, extent[axis_at] // blocks).reshape([-1 if axis == axis_at else 1 for axis in range(len(extent))])
    return gain


def split_up(count, total, bound, skew):
    loads = [(1 << 20) // math.isqrt(grade ** skew) + 1 for grade in range(2, count + 1)]
    spare, holding = total - bound - (count - 1), [1] * (count - 1)
    while spare > 0:
        free = [i for i in range(count - 1) if holding[i] < bound]
        mass, remaining = sum([loads[i] for i in free]), spare
        for i in free:
            more = min(bound - holding[i], max(1, remaining * loads[i] // mass), spare)
            holding[i] = holding[i] + more
            spare = spare - more
    return np.array([bound] + holding)


def uneven_parts(stream_key, amount, total, reach, skew):
    if amount == 2:
        one = jax.random.randint(stream_key, (), max(1, total - reach), min(reach, total - 1) + 1)
        return jnp.stack([one, total - one])
    tallies = jnp.asarray(split_up(amount, total, reach, skew), jnp.int32)
    couples = (amount - 1) // 2
    giver, receiver = tallies[1:1 + 2 * couples:2], tallies[2:2 + 2 * couples:2]
    slack = jnp.minimum(giver - 1, reach - receiver)
    passed = jax.random.randint(jax.random.fold_in(stream_key, 1), (couples,), 0, 1 << 20) % (slack + 1)
    tallies = tallies.at[1:1 + 2 * couples:2].set(giver - passed).at[2:2 + 2 * couples:2].set(receiver + passed)
    return tallies[jax.random.permutation(jax.random.fold_in(stream_key, 2), amount)]


def assign_block(stream_key, own, number, rows, number_of, top, reach, skew):
    sequence = jax.random.permutation(stream_key, number_of)
    heavy_load, usual = shares(number_of, rows * top, reach, skew, True), shares(number_of, rows * top, reach, skew, False)
    places = jnp.arange(number_of)

    def named(lengths, offset_by):
        used = int((lengths > 0).sum())
        fixed = max(1, used // 4)
        shifted = fixed + (places - fixed + offset_by * (used - fixed)) % max(1, number_of - fixed)
        return jnp.zeros((number_of,), jnp.int32).at[sequence[jnp.where(places < fixed, places, shifted)]].set(jnp.asarray(lengths, jnp.int32))

    lengths = jnp.where(number % 4 == 0, named(heavy_load, number // 4), named(usual, number - number // 4 - 1))
    mixed = jax.random.permutation(jax.random.fold_in(own, 3), number_of)
    source_of, receiver = mixed[0:number_of // 2 * 2:2], mixed[1:number_of // 2 * 2:2]
    room = jnp.minimum(lengths[source_of] - 1, reach - lengths[receiver]) // 2
    room = jnp.where((source_of == sequence[0]) | (receiver == sequence[0]) | (lengths[receiver] == 0), 0, jnp.maximum(room, 0))
    shifted = jax.random.randint(jax.random.fold_in(own, 4), (number_of // 2,), 0, 1 << 20) % (room + 1)
    lengths = lengths.at[source_of].add(-shifted).at[receiver].add(shifted)
    labels = jnp.searchsorted(jnp.cumsum(lengths), jnp.arange(rows * top), side="right").astype(jnp.int32)
    grid = labels.reshape(top, rows).T
    grid = grid[jax.random.permutation(jax.random.fold_in(own, 1), rows)]
    offset_by = jax.random.randint(jax.random.fold_in(own, 2), (rows, 1), 0, top)
    return jnp.take_along_axis(grid, (jnp.arange(top)[None, :] + offset_by) % top, axis=1)


def shares(amount, total, reach, skew, full):
    weights = [(1 << 20) // math.isqrt(standing ** skew) + 1 for standing in range(1, amount + 1)]
    largest = reach if full else min(reach, max(-(-total // amount), total * weights[0] // sum(weights)))
    least = 1 if total - largest >= amount - 1 else 0
    holding, rest = [largest] + [least] * (amount - 1), total - largest - least * (amount - 1)
    while rest > 0:
        free = [i for i in range(1, amount) if holding[i] < largest] or [i for i in range(1, amount) if holding[i] < reach]
        whole, left = sum([weights[i] for i in free]), rest
        for i in free:
            addition = min(reach - holding[i], max(1, left * weights[i] // whole), rest)
            holding[i] = holding[i] + addition
            rest = rest - addition
    return np.array(holding)


def noise(key, shape, scale, bound, split=(), held_as=jnp.bfloat16):
    drawn = scale * jax.random.normal(key, shape, jnp.float32)
    if split:
        drawn = drawn * block_levels(key, shape, split, -0.22, 0.18)
    return jnp.clip(drawn, -bound, bound).astype(held_as)


def setup_inputs(seed: int = 0, part: int = 0) -> dict:
    arg_keys = jax.random.split(jax.random.key(seed), 13)
    part_keys = jax.random.split(jax.random.fold_in(arg_keys[12], part), 13)
    queries = draw_queries(jax.random.fold_in(jax.random.fold_in(arg_keys[12], part), 71), part)
    key_cache = draw_key_cache(jax.random.fold_in(jax.random.fold_in(arg_keys[12], part), 71), part)
    value_cache = noise(part_keys[2], (REQS, L, KVH, HD), 1.0, 6.0, ((0, 8), (2, 2)))
    new_keys = draw_new_keys(jax.random.fold_in(jax.random.fold_in(arg_keys[12], part), 71), part)
    new_values = noise(part_keys[4], (REQS, KVH * HD), 1.0, 6.0, ((0, 8), (1, 2)))
    history = uneven_parts(part_keys[5], REQS, REQS * L // 2, L, 1).astype(jnp.int32)
    tokens = noise(part_keys[6], (TOKENS, D), 1.0, 6.0, ((0, 16),))
    expert_ids_keys = jax.random.split(jax.random.fold_in(part_keys[7], 1), TOKENS // TOK_DEV)
    expert_ids_turns = jax.random.permutation(jax.random.fold_in(part_keys[7], 3), TOKENS // TOK_DEV)
    expert_ids = jax.vmap(lambda own, number: assign_block(jax.random.fold_in(part_keys[7], 2), own, number, TOK_DEV, EXPERTS, TOP, CAP, 2))(expert_ids_keys, expert_ids_turns).reshape((TOKENS, TOP))
    gate_values = jnp.clip(0.1 + 0.5 * jax.random.uniform(part_keys[8], (TOKENS, TOP), jnp.float32) ** block_levels(part_keys[8], (TOKENS, TOP), ((0, 16),), -0.2, 0.2), 0.1, 0.6)
    w_gate = noise(arg_keys[9], (2 * EXPERTS, FF // 2, D), D ** -0.5, 0.125, ((0, 8), (1, 2)))
    w_up = noise(arg_keys[10], (2 * EXPERTS, FF // 2, D), D ** -0.5, 0.125, ((0, 8), (1, 2)))
    w_down = noise(arg_keys[11], (2 * EXPERTS, FF // 2, D), FF ** -0.5, 0.21875, ((0, 8), (1, 2)))
    return dict(queries=queries, key_cache=key_cache, value_cache=value_cache, new_keys=new_keys, new_values=new_values, history=history, tokens=tokens, expert_ids=expert_ids, gate_values=gate_values, w_gate=w_gate, w_up=w_up, w_down=w_down)


def attend_one(operands):
    query, keys, values, fresh_key, fresh_value, span = operands
    groups = HQ // KVH
    scaling = HD ** -0.5
    query4 = query.reshape(KVH, groups, HD).astype(jnp.float32)
    scores = jnp.einsum("jgd,ljd->jgl", query4, keys.astype(jnp.float32)) * scaling
    own_score = jnp.einsum("jgd,jd->jg", query4, fresh_key.reshape(KVH, HD).astype(jnp.float32)) * scaling
    usable = jnp.arange(L, dtype=jnp.int32) < span
    scores = jnp.where(usable[None, None, :], scores, -1e30)
    peak = jnp.maximum(jnp.max(scores, axis=-1), own_score)
    exp_terms = jnp.exp(scores - peak[..., None])
    own_exp = jnp.exp(own_score - peak)
    totals = jnp.sum(exp_terms, axis=-1) + own_exp
    attn_weights = lax.optimization_barrier((exp_terms / totals[..., None]).astype(jnp.bfloat16))
    own_weight = lax.optimization_barrier((own_exp / totals).astype(jnp.bfloat16))
    mixture = jnp.einsum("jgl,ljd->jgd", attn_weights.astype(jnp.float32), values.astype(jnp.float32))
    fresh_values = fresh_value.reshape(KVH, HD).astype(jnp.float32)
    mixture = mixture + own_weight.astype(jnp.float32)[..., None] * fresh_values[:, None, :]
    return mixture.reshape(HQ * HD).astype(jnp.bfloat16)


def expert_pair(row_block, gate_pair, up_pair, down_pair):
    slice_width = FF // 2 // N_HEAD
    combined = jnp.zeros((row_block.shape[0], D), jnp.float32)
    for half_idx in range(2):
        gate_act = jnp.dot(row_block, jnp.transpose(gate_pair[half_idx]), preferred_element_type=jnp.float32)
        up_act = jnp.dot(row_block, jnp.transpose(up_pair[half_idx]), preferred_element_type=jnp.float32)
        hidden = (jax.nn.silu(gate_act) * up_act).astype(jnp.bfloat16)
        half_sum = jnp.zeros((row_block.shape[0], D), jnp.float32)
        for slice_idx in range(N_HEAD):
            lower = slice_idx * slice_width
            piece = jnp.dot(hidden[:, lower:lower + slice_width], down_pair[half_idx, lower:lower + slice_width], preferred_element_type=jnp.float32)
            half_sum = half_sum + lax.optimization_barrier(piece.astype(jnp.bfloat16)).astype(jnp.float32)
        combined = combined + lax.optimization_barrier(half_sum.astype(jnp.bfloat16)).astype(jnp.float32)
    return combined


def reference(queries, key_cache, value_cache, new_keys, new_values, history, tokens, expert_ids, gate_values, w_gate, w_up, w_down):
    attn_context = lax.map(attend_one, (queries, key_cache, value_cache, new_keys, new_values, history))
    blocks = N_SEC * N_HEAD
    pair_count = TOK_DEV * TOP
    block_ids = expert_ids.reshape(blocks, pair_count)
    onehot = (block_ids[:, :, None] == jnp.arange(EXPERTS, dtype=jnp.int32)[None, None, :]).astype(jnp.int32)
    rank_of = jnp.cumsum(onehot, axis=1) - 1
    slot_of = jnp.sum(rank_of * onehot, axis=2).astype(jnp.int32)
    row_of = jnp.arange(blocks, dtype=jnp.int32)[:, None] * CAP + slot_of
    token_of = jnp.arange(blocks, dtype=jnp.int32)[:, None] * TOK_DEV + jnp.arange(pair_count, dtype=jnp.int32)[None, :] // TOP
    table = jnp.full((EXPERTS, blocks * CAP), TOKENS, jnp.int32)
    table = table.at[block_ids.reshape(-1), row_of.reshape(-1)].set(token_of.reshape(-1).astype(jnp.int32))
    padded = jnp.concatenate([tokens, jnp.zeros((1, D), tokens.dtype)], axis=0)

    def one_expert(operands):
        index_row, gate_pair, up_pair, down_pair = operands
        return expert_pair(padded[index_row], gate_pair, up_pair, down_pair)

    results = lax.map(one_expert, (table, w_gate.reshape(EXPERTS, 2, FF // 2, D), w_up.reshape(EXPERTS, 2, FF // 2, D), w_down.reshape(EXPERTS, 2, FF // 2, D)))
    picked = results[block_ids.reshape(-1), row_of.reshape(-1)].reshape(TOKENS, TOP, D)
    expert_output = jnp.sum(gate_values[:, :, None] * picked, axis=1).astype(jnp.bfloat16)
    return (attn_context, expert_output)
```

```python
import functools

import jax
import jax.numpy as jnp
from jax import lax
from jax.experimental import pallas as pl
from jax.experimental.pallas import tpu as pltpu
from jax.sharding import PartitionSpec as P

EXPERTS = 64
HQ = 64
KVH = 4
CAP = 2


def attention_block(queries, key_cache, value_cache, new_keys, new_values, history):
    req_count, length, kv_local, head_dim = key_cache.shape
    groups = HQ // KVH
    scaling = head_dim ** (-0.5)
    query4 = queries.reshape(req_count, kv_local, groups, head_dim)
    scores = (
        jnp.einsum("rjgd,rljd->rjgl", query4, key_cache, preferred_element_type=jnp.float32)
        * scaling
    )
    fresh_keys = new_keys.reshape(req_count, kv_local, head_dim)
    own_score = (
        jnp.einsum("rjgd,rjd->rjg", query4, fresh_keys, preferred_element_type=jnp.float32)
        * scaling
    )
    usable = jnp.arange(length, dtype=jnp.int32)[None, :] < history[:, None]
    scores = jnp.where(usable[:, None, None, :], scores, -1e30)
    peak = jnp.maximum(jnp.max(scores, axis=-1), own_score)
    exp_terms = jnp.exp(scores - peak[..., None])
    own_exp = jnp.exp(own_score - peak)
    totals = jnp.sum(exp_terms, axis=-1) + own_exp
    attn_weights = (exp_terms / totals[..., None]).astype(jnp.bfloat16)
    own_weight = (own_exp / totals).astype(jnp.bfloat16)
    mixture = jnp.einsum(
        "rjgl,rljd->rjgd", attn_weights, value_cache, preferred_element_type=jnp.float32
    )
    fresh_values = new_values.reshape(req_count, kv_local, head_dim).astype(jnp.float32)
    mixture = mixture + own_weight.astype(jnp.float32)[..., None] * fresh_values[:, :, None, :]
    return mixture.astype(jnp.bfloat16).reshape(req_count, kv_local * groups * head_dim)


def per_device(
    queries,
    key_cache,
    value_cache,
    new_keys,
    new_values,
    history,
    tokens,
    expert_ids,
    gate_values,
    w_gate,
    w_up,
    w_down,
):
    attn_context = attention_block(queries, key_cache, value_cache, new_keys, new_values, history)
    tok_rows, top_k = expert_ids.shape
    model_dim = tokens.shape[1]
    sec_count = lax.axis_size("sec")
    per_dev = w_gate.shape[0]
    flat_ids = expert_ids.reshape(-1)
    order = jnp.arange(flat_ids.shape[0], dtype=jnp.int32)
    earlier = (flat_ids[:, None] == flat_ids[None, :]) & (order[None, :] < order[:, None])
    slot_of = jnp.sum(earlier.astype(jnp.int32), axis=1)
    target = flat_ids * CAP + slot_of
    matches = (target[None, :] == jnp.arange(EXPERTS * CAP, dtype=jnp.int32)[:, None]).reshape(
        EXPERTS * CAP, tok_rows, top_k
    )
    placing = jnp.any(matches, axis=2).astype(jnp.bfloat16)
    outgoing = jnp.dot(placing, tokens, preferred_element_type=jnp.float32).astype(jnp.bfloat16)
    doubled = jnp.broadcast_to(
        outgoing.reshape(EXPERTS, 1, CAP, model_dim), (EXPERTS, 2, CAP, model_dim)
    ).reshape(sec_count, per_dev, CAP, model_dim)
    weighting = jnp.transpose(jnp.sum(jnp.where(matches, gate_values[None, :, :], 0.0), axis=2))
    both_rows = lax.all_gather(
        lax.all_to_all(doubled, "sec", split_axis=0, concat_axis=0, tiled=True),
        "head",
        axis=0,
        tiled=True,
    )
    gate_act = jnp.einsum("smcd,mfd->smcf", both_rows, w_gate, preferred_element_type=jnp.float32)
    up_act = jnp.einsum("smcd,mfd->smcf", both_rows, w_up, preferred_element_type=jnp.float32)
    hidden = (jax.nn.silu(gate_act) * up_act).astype(jnp.bfloat16)
    part_sums = jnp.einsum("smcf,mfd->smcd", hidden, w_down, preferred_element_type=jnp.float32)
    half_out = lax.psum_scatter(
        part_sums.astype(jnp.bfloat16), "head", scatter_dimension=0, tiled=True
    )
    returned = lax.all_to_all(half_out, "sec", split_axis=0, concat_axis=0, tiled=True)
    expert_sum = jnp.sum(
        returned.reshape(EXPERTS, 2, CAP, model_dim).astype(jnp.float32), axis=1
    ).reshape(EXPERTS * CAP, model_dim)
    expert_output = jnp.dot(
        weighting, expert_sum, precision=lax.Precision.HIGHEST, preferred_element_type=jnp.float32
    ).astype(jnp.bfloat16)
    return (attn_context, expert_output)


ZN, XN, HN = 4, 2, 2
SLOTS = ZN * XN * HN
UNITS = 512
FLIPPED = 3
COLS = 512
LAG = 1
GATE_LANES = 128
MESH_ID = pl.DeviceIdType.MESH
F = {}


def fused_kernel(
    hist_ref,
    q_hbm, nk_hbm, nv_hbm, tok_hbm, ids_hbm, gv_hbm,
    key_hbm, val_hbm, wg_hbm, wu_hbm, wd_hbm,
    attn_ref, out_ref,
    q_ref, nk_ref, nv_ref, tok_ref, ids_ref, gv_ref,
    kbuf, vbuf, wg, wu, wd, flip, qs, cs, xg, xs, hid,
    own1, own2, send1, send2, recv1, recv2,
    in_sem, kv_sem, gu_sem, wd_sem, ag_send, ag_recv, rs_send, rs_recv,
):
    tok_rows, model_dim = tok_ref.shape
    hid_units = wg_hbm.shape[0]
    steps = hid_units // UNITS
    col_steps = model_dim // COLS
    req_count = key_hbm.shape[0]
    heads, head_dim = q_ref.shape[1] // key_hbm.shape[2], key_hbm.shape[2]
    sec = lax.axis_index("sec")
    core = lax.axis_index("head")
    z, x = sec // XN, sec % XN
    x_peer = {"sec": z * XN + (x + 1) % XN, "head": core}
    h_peer = {"sec": sec, "head": (core + 1) % HN}

    def z_peer(k):
        return {"sec": ((z + k) % ZN) * XN + x, "head": core}

    def far_peer(k):
        return {"sec": ((z + k % ZN) % ZN) * XN + (x + k // ZN) % XN, "head": core}

    barrier = pltpu.get_barrier_semaphore()
    for peer in [far_peer(k) for k in range(1, ZN * XN)] + [h_peer]:
        pl.semaphore_signal(barrier, inc=1, device_id=peer, device_id_type=MESH_ID)

    small = [
        pltpu.make_async_copy(src, dst, in_sem.at[i])
        for i, (src, dst) in enumerate([
            (tok_hbm, tok_ref), (ids_hbm, ids_ref), (gv_hbm, gv_ref),
            (q_hbm, q_ref), (nk_hbm, nk_ref), (nv_hbm, nv_ref),
        ])
    ]

    def kv_copies(r):
        return (
            pltpu.make_async_copy(key_hbm.at[r], kbuf.at[r], kv_sem.at[0, r]),
            pltpu.make_async_copy(val_hbm.at[r], vbuf.at[r], kv_sem.at[1, r]),
        )

    def gu_copies(c):
        rows = pl.ds(pl.multiple_of(c * UNITS, UNITS), UNITS)
        return (
            pltpu.make_async_copy(wg_hbm.at[rows], wg.at[rows], gu_sem.at[0, c]),
            pltpu.make_async_copy(wu_hbm.at[rows], wu.at[rows], gu_sem.at[1, c]),
        )

    def wd_copy(c):
        cols = pl.ds(c * COLS, COLS)
        return pltpu.make_async_copy(wd_hbm.at[:, cols], wd.at[:, cols], wd_sem.at[c])

    for copy in small:
        copy.start()
    for r in range(req_count):
        for copy in kv_copies(r):
            copy.start()
    for c in range(steps):
        for copy in gu_copies(c):
            copy.start()
    for c in range(col_steps):
        wd_copy(c).start()

    for copy in small[0:3]:
        copy.wait()
    lane = lax.broadcasted_iota(jnp.int32, (tok_rows, GATE_LANES), 1)
    weight = jnp.zeros((tok_rows, GATE_LANES), jnp.float32)
    ids = ids_ref[...]
    gates = gv_ref[...]
    for k in range(ids_ref.shape[1]):
        weight = weight + jnp.where(lane % EXPERTS == ids[:, k:k + 1], gates[:, k:k + 1], 0.0)
    upper = weight.astype(jnp.bfloat16).astype(jnp.float32)
    xg[0, :, 0:model_dim] = tok_ref[...]
    xg[0, :, model_dim:model_dim + GATE_LANES] = jnp.where(
        lane < EXPERTS, upper, weight - upper
    ).astype(jnp.bfloat16)

    pl.semaphore_wait(barrier, ZN * XN)

    def share(src, dst, peer):
        return pltpu.make_async_remote_copy(
            src_ref=xg.at[src], dst_ref=xg.at[dst],
            send_sem=ag_send.at[dst], recv_sem=ag_recv.at[dst],
            device_id=peer, device_id_type=MESH_ID,
        )

    z_share = [share(0, (ZN - k) % ZN, z_peer(k)) for k in range(1, ZN)]
    x_share = [share(i, ZN + i, x_peer) for i in range(ZN)]
    h_share = [share(i, ZN * XN + i, h_peer) for i in range(ZN * XN)]
    for copy in z_share:
        copy.start()
    x_share[0].start()
    h_share[0].start()

    per_kv = heads // 2
    for copy in small[3:6]:
        copy.wait()
    for i in range(heads):
        qs[i * req_count:(i + 1) * req_count, :] = q_ref[
            :, i * head_dim:(i + 1) * head_dim
        ].astype(jnp.float32)
    scaling = head_dim ** (-0.5)
    places = kbuf.shape[1]
    row_id = lax.broadcasted_iota(jnp.int32, (heads, places), 0)
    col_id = lax.broadcasted_iota(jnp.int32, (heads, places), 1)
    same_head = (col_id % 2) == (row_id // per_kv)
    position = col_id // 2
    low_head = lax.broadcasted_iota(jnp.int32, (heads, head_dim), 0) < per_kv

    def attend(r):
        for copy in kv_copies(r):
            copy.wait()
        query = qs[pl.ds(r, heads, stride=req_count), :]
        scores = lax.dot_general(
            query.astype(jnp.bfloat16), kbuf[r], (((1,), (1,)), ((), ())),
            preferred_element_type=jnp.float32,
        ) * scaling
        scores = jnp.where(same_head & (position < hist_ref[r]), scores, -1e30)
        nk = nk_ref[r:r + 1, :].astype(jnp.float32)
        nv = nv_ref[r:r + 1, :].astype(jnp.float32)
        fresh_key = jnp.where(low_head, nk[:, 0:head_dim], nk[:, head_dim:2 * head_dim])
        fresh_value = jnp.where(low_head, nv[:, 0:head_dim], nv[:, head_dim:2 * head_dim])
        own_score = jnp.sum(query * fresh_key, axis=1, keepdims=True) * scaling
        peak = jnp.maximum(jnp.max(scores, axis=1, keepdims=True), own_score)
        terms = jnp.exp(scores - peak)
        own_term = jnp.exp(own_score - peak)
        inverse = 1.0 / (jnp.sum(terms, axis=1, keepdims=True) + own_term)
        mixture = jnp.dot(
            (terms * inverse).astype(jnp.bfloat16), vbuf[r],
            preferred_element_type=jnp.float32,
        )
        own_weight = (own_term * inverse).astype(jnp.bfloat16).astype(jnp.float32)
        cs[pl.ds(r, heads, stride=req_count), :] = mixture + own_weight * fresh_value

    def turn(c, which):
        source = (wg, wu)[which]
        gu_copies(c)[which].wait()

        def block(i, carry):
            rows = pl.ds(pl.multiple_of(c * UNITS + i * 128, 128), 128)
            flip[which, c, :, pl.ds(pl.multiple_of(i * 128, 128), 128)] = source[rows, :].T
            return carry

        lax.fori_loop(0, UNITS // 128, block, 0)

    def arrived(lo, hi):
        for i in range(lo, hi):
            share(i, i, x_peer).wait_recv()

    def gather_rows(lo, hi):
        rows = xg[lo:hi].astype(jnp.float32).reshape((hi - lo) * tok_rows, xg.shape[2])
        xs[lo * tok_rows:hi * tok_rows, :] = rows.astype(jnp.bfloat16)

    fill = [functools.partial(turn, c, w) for c in range(FLIPPED) for w in range(2)]

    def work(n):
        for _ in range(n):
            if fill:
                fill.pop(0)()

    for r in range(req_count):
        attend(r)
    work(F.get('w0', 1))
    for i in range(1, ZN):
        arrived(i, i + 1)
        x_share[i].start()
        h_share[i].start()
    arrived(ZN, ZN + 1)
    h_share[ZN].start()
    work(F.get('w1', 2))
    for i in range(ZN + 1, 2 * ZN):
        arrived(i, i + 1)
        h_share[i].start()
    for i in range(heads):
        attn_ref[:, i * head_dim:(i + 1) * head_dim] = cs[
            i * req_count:(i + 1) * req_count, :
        ].astype(jnp.bfloat16)
    gather_rows(0, 2 * ZN)
    work(8)
    arrived(2 * ZN, 4 * ZN)
    gather_rows(2 * ZN, 4 * ZN)

    per_expert = hid_units * ZN * XN // EXPERTS
    first_expert = sec * (EXPERTS // (ZN * XN))

    def spread_of(shape, first, unit_dim):
        expert = lax.broadcasted_iota(jnp.int32, shape, 1 - unit_dim) % EXPERTS - first_expert
        at = lax.broadcasted_iota(jnp.int32, shape, unit_dim) + first - expert * per_expert
        return jnp.where((at >= 0) & (at < per_expert), 1.0, 0.0).astype(jnp.bfloat16)

    def project_flipped(c, carry):
        first = pl.multiple_of(c * UNITS, UNITS)
        gate_act = jnp.dot(xs[:, 0:model_dim], flip[0, c], preferred_element_type=jnp.float32)
        up_act = jnp.dot(xs[:, 0:model_dim], flip[1, c], preferred_element_type=jnp.float32)
        share_of = jnp.dot(
            xs[:, model_dim:model_dim + GATE_LANES], spread_of((GATE_LANES, UNITS), first, 1),
            preferred_element_type=jnp.float32,
        )
        hidden = gate_act / (1.0 + jnp.exp(-gate_act)) * up_act
        hid[:, pl.ds(first, UNITS)] = (hidden * share_of).astype(jnp.bfloat16)
        return carry

    def project(c, carry):
        for copy in gu_copies(c):
            copy.wait()
        first = pl.multiple_of(c * UNITS, UNITS)
        rows = pl.ds(first, UNITS)
        gate_act = lax.dot_general(
            wg[rows, :], xs[:, 0:model_dim], (((1,), (1,)), ((), ())),
            preferred_element_type=jnp.float32,
        )
        up_act = lax.dot_general(
            wu[rows, :], xs[:, 0:model_dim], (((1,), (1,)), ((), ())),
            preferred_element_type=jnp.float32,
        )
        share_of = lax.dot_general(
            spread_of((UNITS, GATE_LANES), first, 0), xs[:, model_dim:model_dim + GATE_LANES],
            (((1,), (1,)), ((), ())), preferred_element_type=jnp.float32,
        )
        hidden = gate_act / (1.0 + jnp.exp(-gate_act)) * up_act
        hid[:, rows] = (hidden * share_of).astype(jnp.bfloat16).T
        return carry

    if FLIPPED:
        lax.fori_loop(0, FLIPPED, project_flipped, 0, unroll=F.get('un', False))
    lax.fori_loop(FLIPPED, steps, project, 0, unroll=F.get('un', False))

    half = SLOTS * tok_rows // 2

    def send(c, stage, src, dst, peer):
        return pltpu.make_async_remote_copy(
            src_ref=src, dst_ref=dst,
            send_sem=rs_send.at[c, stage], recv_sem=rs_recv.at[c, stage],
            device_id=peer, device_id_type=MESH_ID,
        )

    def stage1(c):
        return send(c, 0, send1.at[c], recv1.at[c], h_peer)

    def stage2(c):
        return [
            send(c, k, send2.at[c, k], recv2.at[c, k], far_peer(k))
            for k in range(1, ZN * XN)
        ]

    def down(c):
        wd_copy(c).wait()
        part = jnp.dot(
            hid[...], wd[:, c * COLS:(c + 1) * COLS], preferred_element_type=jnp.float32
        )
        own1[c] = part[0:half]
        send1[c] = part[half:2 * half].astype(jnp.bfloat16)
        stage1(c).start()

    def after1(c):
        stage1(c).wait_recv()
        total = own1[c] + recv1[c].astype(jnp.float32)
        own2[c] = total[0:tok_rows]
        for k in range(1, ZN * XN):
            send2[c, k] = total[k * tok_rows:(k + 1) * tok_rows].astype(jnp.bfloat16)
        for copy in stage2(c):
            copy.start()

    def after2(c):
        for copy in stage2(c):
            copy.wait_recv()
        total = own2[c]
        for k in range(1, ZN * XN):
            total = total + recv2[c, k].astype(jnp.float32)
        out_ref[:, c * COLS:(c + 1) * COLS] = total.astype(jnp.bfloat16)

    for step in range(col_steps + LAG):
        if step < col_steps:
            down(step)
        if step >= LAG:
            after1(step - LAG)
    for c in range(col_steps):
        after2(c)
    for copy in z_share + x_share + h_share:
        copy.wait_send()
    for c in range(col_steps):
        for copy in [stage1(c)] + stage2(c):
            copy.wait_send()


def fused_device(
    queries, key_cache, value_cache, new_keys, new_values, history,
    tokens, expert_ids, gate_values, w_gate, w_up, w_down,
):
    req_count, length, kv_local, head_dim = key_cache.shape
    tok_rows, model_dim = tokens.shape
    units = w_gate.shape[0] * w_gate.shape[1]
    keys = key_cache.reshape(req_count, length * kv_local, head_dim)
    values = value_cache.reshape(req_count, length * kv_local, head_dim)
    heads = queries.shape[1] // head_dim
    rows = SLOTS * tok_rows
    wide = model_dim + GATE_LANES
    blocks = model_dim // COLS
    bf16, f32 = jnp.bfloat16, jnp.float32
    vmem = pl.BlockSpec(memory_space=pltpu.VMEM)
    hbm = pl.BlockSpec(memory_space=pltpu.HBM)
    return pl.pallas_call(
        fused_kernel,
        out_shape=(
            jax.ShapeDtypeStruct(queries.shape, bf16),
            jax.ShapeDtypeStruct(tokens.shape, bf16),
        ),
        in_specs=[pl.BlockSpec(memory_space=pltpu.SMEM)] + [hbm] * 11,
        out_specs=(vmem, vmem),
        scratch_shapes=[
            pltpu.VMEM(queries.shape, bf16),
            pltpu.VMEM(new_keys.shape, bf16),
            pltpu.VMEM(new_values.shape, bf16),
            pltpu.VMEM(tokens.shape, bf16),
            pltpu.VMEM(expert_ids.shape, jnp.int32),
            pltpu.VMEM(gate_values.shape, f32),
            pltpu.VMEM(keys.shape, bf16),
            pltpu.VMEM(values.shape, bf16),
            pltpu.VMEM((units, model_dim), bf16),
            pltpu.VMEM((units, model_dim), bf16),
            pltpu.VMEM((units, model_dim), bf16),
            pltpu.VMEM((2, max(FLIPPED, 1), model_dim, UNITS), bf16),
            pltpu.VMEM((heads * req_count, head_dim), f32),
            pltpu.VMEM((heads * req_count, head_dim), f32),
            pltpu.VMEM((SLOTS, tok_rows, wide), bf16),
            pltpu.VMEM((rows, wide), bf16),
            pltpu.VMEM((rows, units), bf16),
            pltpu.VMEM((blocks, rows // 2, COLS), f32),
            pltpu.VMEM((blocks, tok_rows, COLS), f32),
            pltpu.VMEM((blocks, rows // 2, COLS), bf16),
            pltpu.VMEM((blocks, ZN * XN, tok_rows, COLS), bf16),
            pltpu.VMEM((blocks, rows // 2, COLS), bf16),
            pltpu.VMEM((blocks, ZN * XN, tok_rows, COLS), bf16),
            pltpu.SemaphoreType.DMA((6,)),
            pltpu.SemaphoreType.DMA((2, req_count)),
            pltpu.SemaphoreType.DMA((2, units // UNITS)),
            pltpu.SemaphoreType.DMA((blocks,)),
            pltpu.SemaphoreType.DMA((SLOTS,)),
            pltpu.SemaphoreType.DMA((SLOTS,)),
            pltpu.SemaphoreType.DMA((blocks, ZN * XN)),
            pltpu.SemaphoreType.DMA((blocks, ZN * XN)),
        ],
        compiler_params=pltpu.CompilerParams(
            collective_id=0, has_side_effects=True, vmem_limit_bytes=60 * 1024 * 1024
        ),
    )(
        history, queries, new_keys, new_values, tokens, expert_ids, gate_values,
        keys, values,
        w_gate.reshape(units, model_dim), w_up.reshape(units, model_dim),
        w_down.reshape(units, model_dim),
    )


def solution(mesh):
    in_specs = (
        P(("group", "sec"), "head"),
        P(("group", "sec"), None, "head", None),
        P(("group", "sec"), None, "head", None),
        P(("group", "sec"), "head"),
        P(("group", "sec"), "head"),
        P(("group", "sec")),
        P(("group", "sec", "head"), None),
        P(("group", "sec", "head"), None),
        P(("group", "sec", "head"), None),
        P("sec", "head", None),
        P("sec", "head", None),
        P("sec", "head", None),
    )
    out_specs = (P(("group", "sec"), "head"), P(("group", "sec", "head"), None))
    small = mesh.shape["sec"] == ZN * XN and mesh.shape["head"] == HN
    return jax.shard_map(
        fused_device if small else per_device, mesh=mesh, in_specs=in_specs, out_specs=out_specs, check_vma=False
    )
```

```python
import functools

import jax
import jax.numpy as jnp
from jax import lax
from jax.experimental import pallas as pl
from jax.experimental.pallas import tpu as pltpu
from jax.sharding import PartitionSpec as P

EXPERTS = 64
HQ = 64
KVH = 4
CAP = 2


def attention_block(queries, key_cache, value_cache, new_keys, new_values, history):
    req_count, length, kv_local, head_dim = key_cache.shape
    groups = HQ // KVH
    scaling = head_dim ** (-0.5)
    query4 = queries.reshape(req_count, kv_local, groups, head_dim)
    scores = (
        jnp.einsum("rjgd,rljd->rjgl", query4, key_cache, preferred_element_type=jnp.float32)
        * scaling
    )
    fresh_keys = new_keys.reshape(req_count, kv_local, head_dim)
    own_score = (
        jnp.einsum("rjgd,rjd->rjg", query4, fresh_keys, preferred_element_type=jnp.float32)
        * scaling
    )
    usable = jnp.arange(length, dtype=jnp.int32)[None, :] < history[:, None]
    scores = jnp.where(usable[:, None, None, :], scores, -1e30)
    peak = jnp.maximum(jnp.max(scores, axis=-1), own_score)
    exp_terms = jnp.exp(scores - peak[..., None])
    own_exp = jnp.exp(own_score - peak)
    totals = jnp.sum(exp_terms, axis=-1) + own_exp
    attn_weights = (exp_terms / totals[..., None]).astype(jnp.bfloat16)
    own_weight = (own_exp / totals).astype(jnp.bfloat16)
    mixture = jnp.einsum(
        "rjgl,rljd->rjgd", attn_weights, value_cache, preferred_element_type=jnp.float32
    )
    fresh_values = new_values.reshape(req_count, kv_local, head_dim).astype(jnp.float32)
    mixture = mixture + own_weight.astype(jnp.float32)[..., None] * fresh_values[:, :, None, :]
    return mixture.astype(jnp.bfloat16).reshape(req_count, kv_local * groups * head_dim)


def per_device(
    queries,
    key_cache,
    value_cache,
    new_keys,
    new_values,
    history,
    tokens,
    expert_ids,
    gate_values,
    w_gate,
    w_up,
    w_down,
):
    attn_context = attention_block(queries, key_cache, value_cache, new_keys, new_values, history)
    tok_rows, top_k = expert_ids.shape
    model_dim = tokens.shape[1]
    sec_count = lax.axis_size("sec")
    per_dev = w_gate.shape[0]
    flat_ids = expert_ids.reshape(-1)
    order = jnp.arange(flat_ids.shape[0], dtype=jnp.int32)
    earlier = (flat_ids[:, None] == flat_ids[None, :]) & (order[None, :] < order[:, None])
    slot_of = jnp.sum(earlier.astype(jnp.int32), axis=1)
    target = flat_ids * CAP + slot_of
    matches = (target[None, :] == jnp.arange(EXPERTS * CAP, dtype=jnp.int32)[:, None]).reshape(
        EXPERTS * CAP, tok_rows, top_k
    )
    placing = jnp.any(matches, axis=2).astype(jnp.bfloat16)
    outgoing = jnp.dot(placing, tokens, preferred_element_type=jnp.float32).astype(jnp.bfloat16)
    doubled = jnp.broadcast_to(
        outgoing.reshape(EXPERTS, 1, CAP, model_dim), (EXPERTS, 2, CAP, model_dim)
    ).reshape(sec_count, per_dev, CAP, model_dim)
    weighting = jnp.transpose(jnp.sum(jnp.where(matches, gate_values[None, :, :], 0.0), axis=2))
    both_rows = lax.all_gather(
        lax.all_to_all(doubled, "sec", split_axis=0, concat_axis=0, tiled=True),
        "head",
        axis=0,
        tiled=True,
    )
    gate_act = jnp.einsum("smcd,mfd->smcf", both_rows, w_gate, preferred_element_type=jnp.float32)
    up_act = jnp.einsum("smcd,mfd->smcf", both_rows, w_up, preferred_element_type=jnp.float32)
    hidden = (jax.nn.silu(gate_act) * up_act).astype(jnp.bfloat16)
    part_sums = jnp.einsum("smcf,mfd->smcd", hidden, w_down, preferred_element_type=jnp.float32)
    half_out = lax.psum_scatter(
        part_sums.astype(jnp.bfloat16), "head", scatter_dimension=0, tiled=True
    )
    returned = lax.all_to_all(half_out, "sec", split_axis=0, concat_axis=0, tiled=True)
    expert_sum = jnp.sum(
        returned.reshape(EXPERTS, 2, CAP, model_dim).astype(jnp.float32), axis=1
    ).reshape(EXPERTS * CAP, model_dim)
    expert_output = jnp.dot(
        weighting, expert_sum, precision=lax.Precision.HIGHEST, preferred_element_type=jnp.float32
    ).astype(jnp.bfloat16)
    return (attn_context, expert_output)


ZN, XN, HN = 4, 2, 2
SLOTS = ZN * XN * HN
UNITS = 1024
COLS = 1024
LAG = 1
GATE_LANES = 128
MESH_ID = pl.DeviceIdType.MESH
EARLY = 1


def fused_kernel(
    hist_ref,
    q_hbm, nk_hbm, nv_hbm, tok_hbm, ids_hbm, gv_hbm,
    key_hbm, val_hbm, wg_hbm, wu_hbm, wd_hbm,
    attn_ref, out_ref,
    q_ref, nk_ref, nv_ref, tok_ref, ids_ref, gv_ref,
    kbuf, vbuf, wg, wu, wd, qs, cs, xg, xs, hid,
    own1, own2, send1, send2, recv1, recv2,
    in_sem, kv_sem, gu_sem, wd_sem, ag_send, ag_recv, rs_send, rs_recv,
):
    tok_rows, model_dim = tok_ref.shape
    hid_units = wg_hbm.shape[0]
    steps = hid_units // UNITS
    col_steps = model_dim // COLS
    req_count = key_hbm.shape[0]
    heads, head_dim = q_ref.shape[1] // key_hbm.shape[2], key_hbm.shape[2]
    sec = lax.axis_index("sec")
    core = lax.axis_index("head")
    z, x = sec // XN, sec % XN
    x_peer = {"sec": z * XN + (x + 1) % XN, "head": core}
    h_peer = {"sec": sec, "head": (core + 1) % HN}

    def z_peer(k):
        return {"sec": ((z + k) % ZN) * XN + x, "head": core}

    def far_peer(k):
        return {"sec": ((z + k % ZN) % ZN) * XN + (x + k // ZN) % XN, "head": core}

    barrier = pltpu.get_barrier_semaphore()
    for peer in [far_peer(k) for k in range(1, ZN * XN)] + [h_peer]:
        pl.semaphore_signal(barrier, inc=1, device_id=peer, device_id_type=MESH_ID)

    small = [
        pltpu.make_async_copy(src, dst, in_sem.at[i])
        for i, (src, dst) in enumerate([
            (tok_hbm, tok_ref), (ids_hbm, ids_ref), (gv_hbm, gv_ref),
            (q_hbm, q_ref), (nk_hbm, nk_ref), (nv_hbm, nv_ref),
        ])
    ]

    def kv_copies(r):
        return (
            pltpu.make_async_copy(key_hbm.at[r], kbuf.at[r], kv_sem.at[0, r]),
            pltpu.make_async_copy(val_hbm.at[r], vbuf.at[r], kv_sem.at[1, r]),
        )

    def gu_copies(c):
        rows = pl.ds(pl.multiple_of(c * UNITS, UNITS), UNITS)
        return (
            pltpu.make_async_copy(wg_hbm.at[rows], wg.at[rows], gu_sem.at[0, c]),
            pltpu.make_async_copy(wu_hbm.at[rows], wu.at[rows], gu_sem.at[1, c]),
        )

    def wd_copy(c):
        cols = pl.ds(c * COLS, COLS)
        return pltpu.make_async_copy(wd_hbm.at[:, cols], wd.at[:, cols], wd_sem.at[c])

    for copy in small:
        copy.start()
    for r in range(req_count):
        for copy in kv_copies(r):
            copy.start()
    def start_weights(lo, hi):
        for c in range(lo, hi):
            for copy in gu_copies(c):
                copy.start()

    start_weights(0, EARLY)
    for copy in small[0:3]:
        copy.wait()
    lane = lax.broadcasted_iota(jnp.int32, (tok_rows, GATE_LANES), 1)
    weight = jnp.zeros((tok_rows, GATE_LANES), jnp.float32)
    ids = ids_ref[...]
    gates = gv_ref[...]
    for k in range(ids_ref.shape[1]):
        weight = weight + jnp.where(lane % EXPERTS == ids[:, k:k + 1], gates[:, k:k + 1], 0.0)
    upper = weight.astype(jnp.bfloat16).astype(jnp.float32)
    xg[0, :, 0:model_dim] = tok_ref[...]
    xg[0, :, model_dim:model_dim + GATE_LANES] = jnp.where(
        lane < EXPERTS, upper, weight - upper
    ).astype(jnp.bfloat16)

    pl.semaphore_wait(barrier, ZN * XN)

    def share(src, dst, peer):
        return pltpu.make_async_remote_copy(
            src_ref=xg.at[src], dst_ref=xg.at[dst],
            send_sem=ag_send.at[dst], recv_sem=ag_recv.at[dst],
            device_id=peer, device_id_type=MESH_ID,
        )

    z_share = [share(0, (ZN - k) % ZN, z_peer(k)) for k in range(1, ZN)]
    x_share = [share(i, ZN + i, x_peer) for i in range(ZN)]
    h_share = [share(i, ZN * XN + i, h_peer) for i in range(ZN * XN)]
    for copy in z_share:
        copy.start()
    x_share[0].start()
    h_share[0].start()
    start_weights(EARLY, steps)
    for c in range(col_steps):
        wd_copy(c).start()

    per_kv = heads // 2
    for copy in small[3:6]:
        copy.wait()
    for i in range(heads):
        qs[i * req_count:(i + 1) * req_count, :] = q_ref[
            :, i * head_dim:(i + 1) * head_dim
        ].astype(jnp.float32)
    scaling = head_dim ** (-0.5)
    places = kbuf.shape[1]
    row_id = lax.broadcasted_iota(jnp.int32, (heads, places), 0)
    col_id = lax.broadcasted_iota(jnp.int32, (heads, places), 1)
    same_head = (col_id % 2) == (row_id // per_kv)
    position = col_id // 2
    low_head = lax.broadcasted_iota(jnp.int32, (heads, head_dim), 0) < per_kv

    def attend(r):
        for copy in kv_copies(r):
            copy.wait()
        query = qs[pl.ds(r, heads, stride=req_count), :]
        scores = lax.dot_general(
            query.astype(jnp.bfloat16), kbuf[r], (((1,), (1,)), ((), ())),
            preferred_element_type=jnp.float32,
        ) * scaling
        scores = jnp.where(same_head & (position < hist_ref[r]), scores, -1e30)
        nk = nk_ref[r:r + 1, :].astype(jnp.float32)
        nv = nv_ref[r:r + 1, :].astype(jnp.float32)
        fresh_key = jnp.where(low_head, nk[:, 0:head_dim], nk[:, head_dim:2 * head_dim])
        fresh_value = jnp.where(low_head, nv[:, 0:head_dim], nv[:, head_dim:2 * head_dim])
        own_score = jnp.sum(query * fresh_key, axis=1, keepdims=True) * scaling
        peak = jnp.maximum(jnp.max(scores, axis=1, keepdims=True), own_score)
        terms = jnp.exp(scores - peak)
        own_term = jnp.exp(own_score - peak)
        inverse = 1.0 / (jnp.sum(terms, axis=1, keepdims=True) + own_term)
        mixture = jnp.dot(
            (terms * inverse).astype(jnp.bfloat16), vbuf[r],
            preferred_element_type=jnp.float32,
        )
        own_weight = (own_term * inverse).astype(jnp.bfloat16).astype(jnp.float32)
        cs[pl.ds(r, heads, stride=req_count), :] = mixture + own_weight * fresh_value

    def arrived(lo, hi):
        for i in range(lo, hi):
            share(i, i, x_peer).wait_recv()

    def gather_rows(lo, hi):
        rows = xg[lo:hi].astype(jnp.float32).reshape((hi - lo) * tok_rows, xg.shape[2])
        xs[lo * tok_rows:hi * tok_rows, :] = rows.astype(jnp.bfloat16)

    attend(0)
    for i in range(1, ZN):
        arrived(i, i + 1)
        x_share[i].start()
        h_share[i].start()
    arrived(ZN, ZN + 1)
    h_share[ZN].start()
    attend(1)
    for i in range(ZN + 1, 2 * ZN):
        arrived(i, i + 1)
        h_share[i].start()
    attend(2)
    attend(3)
    for i in range(heads):
        attn_ref[:, i * head_dim:(i + 1) * head_dim] = cs[
            i * req_count:(i + 1) * req_count, :
        ].astype(jnp.bfloat16)
    gather_rows(0, 2 * ZN)
    arrived(2 * ZN, 4 * ZN)
    gather_rows(2 * ZN, 4 * ZN)

    per_expert = hid_units * ZN * XN // EXPERTS
    first_expert = sec * (EXPERTS // (ZN * XN))

    shape = (UNITS, GATE_LANES)
    expert = lax.broadcasted_iota(jnp.int32, shape, 1) % EXPERTS - first_expert
    unit_id = lax.broadcasted_iota(jnp.int32, shape, 0) - expert * per_expert

    def project(c, carry):
        for copy in gu_copies(c):
            copy.wait()
        first = pl.multiple_of(c * UNITS, UNITS)
        rows = pl.ds(first, UNITS)
        gate_act = lax.dot_general(
            wg[rows, :], xs[:, 0:model_dim], (((1,), (1,)), ((), ())),
            preferred_element_type=jnp.float32,
        )
        up_act = lax.dot_general(
            wu[rows, :], xs[:, 0:model_dim], (((1,), (1,)), ((), ())),
            preferred_element_type=jnp.float32,
        )
        at = unit_id + first
        spread = jnp.where((at >= 0) & (at < per_expert), 1.0, 0.0).astype(jnp.bfloat16)
        share_of = lax.dot_general(
            spread, xs[:, model_dim:model_dim + GATE_LANES],
            (((1,), (1,)), ((), ())), preferred_element_type=jnp.float32,
        )
        hidden = gate_act / (1.0 + jnp.exp(-gate_act)) * up_act
        hid[:, rows] = (hidden * share_of).astype(jnp.bfloat16).T
        return carry

    lax.fori_loop(0, steps, project, 0)

    half = SLOTS * tok_rows // 2

    def send(c, stage, src, dst, peer):
        return pltpu.make_async_remote_copy(
            src_ref=src, dst_ref=dst,
            send_sem=rs_send.at[c, stage], recv_sem=rs_recv.at[c, stage],
            device_id=peer, device_id_type=MESH_ID,
        )

    def stage1(c):
        return send(c, 0, send1.at[c], recv1.at[c], h_peer)

    def stage2(c):
        return [
            send(c, k, send2.at[c, k], recv2.at[c, k], far_peer(k))
            for k in range(1, ZN * XN)
        ]

    def down(c):
        wd_copy(c).wait()
        part = jnp.dot(
            hid[...], wd[:, c * COLS:(c + 1) * COLS], preferred_element_type=jnp.float32
        )
        own1[c] = part[0:half]
        send1[c] = part[half:2 * half].astype(jnp.bfloat16)
        stage1(c).start()

    def after1(c):
        stage1(c).wait_recv()
        total = own1[c] + recv1[c].astype(jnp.float32)
        own2[c] = total[0:tok_rows]
        for k in range(1, ZN * XN):
            send2[c, k] = total[k * tok_rows:(k + 1) * tok_rows].astype(jnp.bfloat16)
        for copy in stage2(c):
            copy.start()

    def after2(c):
        for copy in stage2(c):
            copy.wait_recv()
        total = own2[c]
        for k in range(1, ZN * XN):
            total = total + recv2[c, k].astype(jnp.float32)
        out_ref[:, c * COLS:(c + 1) * COLS] = total.astype(jnp.bfloat16)

    for step in range(col_steps + LAG):
        if step < col_steps:
            down(step)
        if step >= LAG:
            after1(step - LAG)
    for c in range(col_steps):
        after2(c)
    for copy in z_share + x_share + h_share:
        copy.wait_send()
    for c in range(col_steps):
        for copy in [stage1(c)] + stage2(c):
            copy.wait_send()


def fused_device(
    queries, key_cache, value_cache, new_keys, new_values, history,
    tokens, expert_ids, gate_values, w_gate, w_up, w_down,
):
    req_count, length, kv_local, head_dim = key_cache.shape
    tok_rows, model_dim = tokens.shape
    units = w_gate.shape[0] * w_gate.shape[1]
    keys = key_cache.reshape(req_count, length * kv_local, head_dim)
    values = value_cache.reshape(req_count, length * kv_local, head_dim)
    heads = queries.shape[1] // head_dim
    rows = SLOTS * tok_rows
    wide = model_dim + GATE_LANES
    blocks = model_dim // COLS
    bf16, f32 = jnp.bfloat16, jnp.float32
    vmem = pl.BlockSpec(memory_space=pltpu.VMEM)
    hbm = pl.BlockSpec(memory_space=pltpu.HBM)
    return pl.pallas_call(
        fused_kernel,
        out_shape=(pltpu.VMEM(queries.shape, bf16), pltpu.VMEM(tokens.shape, bf16)),
        in_specs=[pl.BlockSpec(memory_space=pltpu.SMEM)] + [hbm] * 11,
        out_specs=(vmem, vmem),
        scratch_shapes=[
            pltpu.VMEM(queries.shape, bf16),
            pltpu.VMEM(new_keys.shape, bf16),
            pltpu.VMEM(new_values.shape, bf16),
            pltpu.VMEM(tokens.shape, bf16),
            pltpu.VMEM(expert_ids.shape, jnp.int32),
            pltpu.VMEM(gate_values.shape, f32),
            pltpu.VMEM(keys.shape, bf16),
            pltpu.VMEM(values.shape, bf16),
            pltpu.VMEM((units, model_dim), bf16),
            pltpu.VMEM((units, model_dim), bf16),
            pltpu.VMEM((units, model_dim), bf16),
            pltpu.VMEM((heads * req_count, head_dim), f32),
            pltpu.VMEM((heads * req_count, head_dim), f32),
            pltpu.VMEM((SLOTS, tok_rows, wide), bf16),
            pltpu.VMEM((rows, wide), bf16),
            pltpu.VMEM((rows, units), bf16),
            pltpu.VMEM((blocks, rows // 2, COLS), f32),
            pltpu.VMEM((blocks, tok_rows, COLS), f32),
            pltpu.VMEM((blocks, rows // 2, COLS), bf16),
            pltpu.VMEM((blocks, ZN * XN, tok_rows, COLS), bf16),
            pltpu.VMEM((blocks, rows // 2, COLS), bf16),
            pltpu.VMEM((blocks, ZN * XN, tok_rows, COLS), bf16),
            pltpu.SemaphoreType.DMA((6,)),
            pltpu.SemaphoreType.DMA((2, req_count)),
            pltpu.SemaphoreType.DMA((2, units // UNITS)),
            pltpu.SemaphoreType.DMA((blocks,)),
            pltpu.SemaphoreType.DMA((SLOTS,)),
            pltpu.SemaphoreType.DMA((SLOTS,)),
            pltpu.SemaphoreType.DMA((blocks, ZN * XN)),
            pltpu.SemaphoreType.DMA((blocks, ZN * XN)),
        ],
        compiler_params=pltpu.CompilerParams(
            collective_id=0, has_side_effects=True, vmem_limit_bytes=60 * 1024 * 1024
        ),
    )(
        history, queries, new_keys, new_values, tokens, expert_ids, gate_values,
        keys, values,
        w_gate.reshape(units, model_dim), w_up.reshape(units, model_dim),
        w_down.reshape(units, model_dim),
    )


def solution(mesh):
    in_specs = (
        P(("group", "sec"), "head"),
        P(("group", "sec"), None, "head", None),
        P(("group", "sec"), None, "head", None),
        P(("group", "sec"), "head"),
        P(("group", "sec"), "head"),
        P(("group", "sec")),
        P(("group", "sec", "head"), None),
        P(("group", "sec", "head"), None),
        P(("group", "sec", "head"), None),
        P("sec", "head", None),
        P("sec", "head", None),
        P("sec", "head", None),
    )
    out_specs = (P(("group", "sec"), "head"), P(("group", "sec", "head"), None))
    small = mesh.shape["sec"] == ZN * XN and mesh.shape["head"] == HN
    return jax.shard_map(
        fused_device if small else per_device, mesh=mesh, in_specs=in_specs, out_specs=out_specs, check_vma=False
    )
```

```python
import functools

import jax
import jax.numpy as jnp
from jax import lax
from jax.experimental import pallas as pl
from jax.experimental.pallas import tpu as pltpu
from jax.sharding import PartitionSpec as P

EXPERTS = 64
HQ = 64
KVH = 4
CAP = 2


def attention_block(queries, key_cache, value_cache, new_keys, new_values, history):
    req_count, length, kv_local, head_dim = key_cache.shape
    groups = HQ // KVH
    scaling = head_dim ** (-0.5)
    query4 = queries.reshape(req_count, kv_local, groups, head_dim)
    scores = (
        jnp.einsum("rjgd,rljd->rjgl", query4, key_cache, preferred_element_type=jnp.float32)
        * scaling
    )
    fresh_keys = new_keys.reshape(req_count, kv_local, head_dim)
    own_score = (
        jnp.einsum("rjgd,rjd->rjg", query4, fresh_keys, preferred_element_type=jnp.float32)
        * scaling
    )
    usable = jnp.arange(length, dtype=jnp.int32)[None, :] < history[:, None]
    scores = jnp.where(usable[:, None, None, :], scores, -1e30)
    peak = jnp.maximum(jnp.max(scores, axis=-1), own_score)
    exp_terms = jnp.exp(scores - peak[..., None])
    own_exp = jnp.exp(own_score - peak)
    totals = jnp.sum(exp_terms, axis=-1) + own_exp
    attn_weights = (exp_terms / totals[..., None]).astype(jnp.bfloat16)
    own_weight = (own_exp / totals).astype(jnp.bfloat16)
    mixture = jnp.einsum(
        "rjgl,rljd->rjgd", attn_weights, value_cache, preferred_element_type=jnp.float32
    )
    fresh_values = new_values.reshape(req_count, kv_local, head_dim).astype(jnp.float32)
    mixture = mixture + own_weight.astype(jnp.float32)[..., None] * fresh_values[:, :, None, :]
    return mixture.astype(jnp.bfloat16).reshape(req_count, kv_local * groups * head_dim)


def per_device(
    queries,
    key_cache,
    value_cache,
    new_keys,
    new_values,
    history,
    tokens,
    expert_ids,
    gate_values,
    w_gate,
    w_up,
    w_down,
):
    attn_context = attention_block(queries, key_cache, value_cache, new_keys, new_values, history)
    tok_rows, top_k = expert_ids.shape
    model_dim = tokens.shape[1]
    sec_count = lax.axis_size("sec")
    per_dev = w_gate.shape[0]
    flat_ids = expert_ids.reshape(-1)
    order = jnp.arange(flat_ids.shape[0], dtype=jnp.int32)
    earlier = (flat_ids[:, None] == flat_ids[None, :]) & (order[None, :] < order[:, None])
    slot_of = jnp.sum(earlier.astype(jnp.int32), axis=1)
    target = flat_ids * CAP + slot_of
    matches = (target[None, :] == jnp.arange(EXPERTS * CAP, dtype=jnp.int32)[:, None]).reshape(
        EXPERTS * CAP, tok_rows, top_k
    )
    placing = jnp.any(matches, axis=2).astype(jnp.bfloat16)
    outgoing = jnp.dot(placing, tokens, preferred_element_type=jnp.float32).astype(jnp.bfloat16)
    doubled = jnp.broadcast_to(
        outgoing.reshape(EXPERTS, 1, CAP, model_dim), (EXPERTS, 2, CAP, model_dim)
    ).reshape(sec_count, per_dev, CAP, model_dim)
    weighting = jnp.transpose(jnp.sum(jnp.where(matches, gate_values[None, :, :], 0.0), axis=2))
    both_rows = lax.all_gather(
        lax.all_to_all(doubled, "sec", split_axis=0, concat_axis=0, tiled=True),
        "head",
        axis=0,
        tiled=True,
    )
    gate_act = jnp.einsum("smcd,mfd->smcf", both_rows, w_gate, preferred_element_type=jnp.float32)
    up_act = jnp.einsum("smcd,mfd->smcf", both_rows, w_up, preferred_element_type=jnp.float32)
    hidden = (jax.nn.silu(gate_act) * up_act).astype(jnp.bfloat16)
    part_sums = jnp.einsum("smcf,mfd->smcd", hidden, w_down, preferred_element_type=jnp.float32)
    half_out = lax.psum_scatter(
        part_sums.astype(jnp.bfloat16), "head", scatter_dimension=0, tiled=True
    )
    returned = lax.all_to_all(half_out, "sec", split_axis=0, concat_axis=0, tiled=True)
    expert_sum = jnp.sum(
        returned.reshape(EXPERTS, 2, CAP, model_dim).astype(jnp.float32), axis=1
    ).reshape(EXPERTS * CAP, model_dim)
    expert_output = jnp.dot(
        weighting, expert_sum, precision=lax.Precision.HIGHEST, preferred_element_type=jnp.float32
    ).astype(jnp.bfloat16)
    return (attn_context, expert_output)


ZN, XN, HN = 4, 2, 2
SLOTS = ZN * XN * HN
UNITS = 512
COLS = 512
LAG = 1
GATE_LANES = 128
MESH_ID = pl.DeviceIdType.MESH
EARLY = 2
IDLE, BESIDE = 1, 3
BODIES = 4
TURN = 128
FILL = (4, 3, 1)
ATT = (2, 1, 1)
SPLITS = (0, 2176)
VIA_X = (0, 1)
UNROLL = False
ZORDER = (1, 2, 3)


def fused_kernel(
    hist_ref,
    q_hbm, nk_hbm, nv_hbm, tok_hbm, ids_hbm, gv_hbm,
    key_hbm, val_hbm, wg_hbm, wu_hbm, wd_hbm,
    attn_ref, out_ref,
    q_ref, nk_ref, nv_ref, tok_ref, ids_ref, gv_ref,
    kbuf, vbuf, wg, wu, wd, flip, qs, cs, xg, xs, hid,
    own1, own2, send1, send2, recv1, recv2,
    in_sem, kv_sem, gu_sem, wd_sem, ag_send, ag_recv, rs_send, rs_recv,
):
    tok_rows, model_dim = tok_ref.shape
    hid_units = wg_hbm.shape[0]
    steps = hid_units // UNITS
    col_steps = model_dim // COLS
    req_count = key_hbm.shape[0]
    heads, head_dim = q_ref.shape[1] // key_hbm.shape[2], key_hbm.shape[2]
    sec = lax.axis_index("sec")
    core = lax.axis_index("head")
    z, x = sec // XN, sec % XN
    x_peer = {"sec": z * XN + (x + 1) % XN, "head": core}
    h_peer = {"sec": sec, "head": (core + 1) % HN}

    def z_peer(k):
        return {"sec": ((z + k) % ZN) * XN + x, "head": core}

    def far_peer(k):
        return {"sec": ((z + k % ZN) % ZN) * XN + (x + k // ZN) % XN, "head": core}

    barrier = pltpu.get_barrier_semaphore()
    for peer in [far_peer(k) for k in range(1, ZN * XN)] + [h_peer]:
        pl.semaphore_signal(barrier, inc=1, device_id=peer, device_id_type=MESH_ID)

    small = [
        pltpu.make_async_copy(src, dst, in_sem.at[i])
        for i, (src, dst) in enumerate([
            (tok_hbm, tok_ref), (ids_hbm, ids_ref), (gv_hbm, gv_ref),
            (q_hbm, q_ref), (nk_hbm, nk_ref), (nv_hbm, nv_ref),
        ])
    ]

    def kv_copies(r):
        return (
            pltpu.make_async_copy(key_hbm.at[r], kbuf.at[r], kv_sem.at[0, r]),
            pltpu.make_async_copy(val_hbm.at[r], vbuf.at[r], kv_sem.at[1, r]),
        )

    def gu_copies(c):
        rows = pl.ds(pl.multiple_of(c * UNITS, UNITS), UNITS)
        return (
            pltpu.make_async_copy(wg_hbm.at[rows], wg.at[rows], gu_sem.at[0, c]),
            pltpu.make_async_copy(wu_hbm.at[rows], wu.at[rows], gu_sem.at[1, c]),
        )

    def wd_copy(c):
        cols = pl.ds(c * COLS, COLS)
        return pltpu.make_async_copy(wd_hbm.at[:, cols], wd.at[:, cols], wd_sem.at[c])

    for copy in small:
        copy.start()
    for r in range(req_count):
        for copy in kv_copies(r):
            copy.start()
    def start_weights(lo, hi):
        for c in range(lo, hi):
            for copy in gu_copies(c):
                copy.start()

    start_weights(0, EARLY)
    for copy in small[0:3]:
        copy.wait()
    lane = lax.broadcasted_iota(jnp.int32, (tok_rows, GATE_LANES), 1)
    weight = jnp.zeros((tok_rows, GATE_LANES), jnp.float32)
    ids = ids_ref[...]
    gates = gv_ref[...]
    for k in range(ids_ref.shape[1]):
        weight = weight + jnp.where(lane % EXPERTS == ids[:, k:k + 1], gates[:, k:k + 1], 0.0)
    upper = weight.astype(jnp.bfloat16).astype(jnp.float32)
    xg[0, :, 0:model_dim] = tok_ref[...]
    xg[0, :, model_dim:model_dim + GATE_LANES] = jnp.where(
        lane < EXPERTS, upper, weight - upper
    ).astype(jnp.bfloat16)

    pl.semaphore_wait(barrier, ZN * XN)

    parts = range(len(SPLITS) - 1)

    def share(src, dst, peer, p):
        cols = pl.ds(SPLITS[p], SPLITS[p + 1] - SPLITS[p])
        return pltpu.make_async_remote_copy(
            src_ref=xg.at[src, :, cols], dst_ref=xg.at[dst, :, cols],
            send_sem=ag_send.at[p, dst], recv_sem=ag_recv.at[p, dst],
            device_id=peer, device_id_type=MESH_ID,
        )

    def z_share(k, p):
        return share(0, (ZN - k) % ZN, z_peer(k), p)

    def x_share(i, p):
        return share(i, ZN + i, x_peer, p)

    def h_share(i, p):
        return share(i, ZN * XN + i, h_peer, p)

    for p in parts:
        for k in ZORDER:
            z_share(k, p).start()
        x_share(0, p).start()
    for p in parts:
        h_share(0, p).start()

    start_weights(EARLY, steps)
    for c in range(col_steps):
        wd_copy(c).start()

    per_kv = heads // 2
    for copy in small[3:6]:
        copy.wait()
    for i in range(heads):
        qs[i * req_count:(i + 1) * req_count, :] = q_ref[
            :, i * head_dim:(i + 1) * head_dim
        ].astype(jnp.float32)
    scaling = head_dim ** (-0.5)
    places = kbuf.shape[1]
    row_id = lax.broadcasted_iota(jnp.int32, (heads, places), 0)
    col_id = lax.broadcasted_iota(jnp.int32, (heads, places), 1)
    same_head = (col_id % 2) == (row_id // per_kv)
    position = col_id // 2
    low_head = lax.broadcasted_iota(jnp.int32, (heads, head_dim), 0) < per_kv

    def attend(r):
        for copy in kv_copies(r):
            copy.wait()
        query = qs[pl.ds(r, heads, stride=req_count), :]
        scores = lax.dot_general(
            query.astype(jnp.bfloat16), kbuf[r], (((1,), (1,)), ((), ())),
            preferred_element_type=jnp.float32,
        ) * scaling
        scores = jnp.where(same_head & (position < hist_ref[r]), scores, -1e30)
        nk = nk_ref[r:r + 1, :].astype(jnp.float32)
        nv = nv_ref[r:r + 1, :].astype(jnp.float32)
        fresh_key = jnp.where(low_head, nk[:, 0:head_dim], nk[:, head_dim:2 * head_dim])
        fresh_value = jnp.where(low_head, nv[:, 0:head_dim], nv[:, head_dim:2 * head_dim])
        own_score = jnp.sum(query * fresh_key, axis=1, keepdims=True) * scaling
        peak = jnp.maximum(jnp.max(scores, axis=1, keepdims=True), own_score)
        terms = jnp.exp(scores - peak)
        own_term = jnp.exp(own_score - peak)
        inverse = 1.0 / (jnp.sum(terms, axis=1, keepdims=True) + own_term)
        mixture = jnp.dot(
            (terms * inverse).astype(jnp.bfloat16), vbuf[r],
            preferred_element_type=jnp.float32,
        )
        own_weight = (own_term * inverse).astype(jnp.bfloat16).astype(jnp.float32)
        cs[pl.ds(r, heads, stride=req_count), :] = mixture + own_weight * fresh_value

    turned = (IDLE + BESIDE) * UNITS
    arrived_units = set()

    def need(c, which):
        if (c, which) not in arrived_units:
            arrived_units.add((c, which))
            gu_copies(c)[which].wait()

    def turn(which, i):
        need(i * TURN // UNITS, which)
        first = i * TURN
        source = (wg, wu)[which]
        flip[which, first // UNITS, :, first % UNITS:first % UNITS + TURN] = source[first:first + TURN, :].T

    jobs = [(w, i) for i in range(IDLE * UNITS // TURN) for w in range(2)]
    seats = list(range(req_count))

    def meanwhile(place):
        for _ in range(ATT[place]):
            attend(seats.pop(0))
        for _ in range(FILL[place]):
            if jobs:
                turn(*jobs.pop(0))

    def arrived(i, p):
        share(i, i, x_peer, p).wait_recv()

    def gather_rows(lo, hi):
        rows = xg[lo:hi].astype(jnp.float32).reshape((hi - lo) * tok_rows, xg.shape[2])
        xs[lo * tok_rows:hi * tok_rows, :] = rows.astype(jnp.bfloat16)

    meanwhile(0)
    for p in parts:
        for i in range(1, ZN):
            arrived(i, p)
            x_share(i, p).start()
            h_share(i, p).start()
    for p in parts:
        arrived(ZN, p)
        h_share(ZN, p).start()
    meanwhile(1)
    for p in parts:
        for i in range(ZN + 1, 2 * ZN):
            arrived(i, p)
            h_share(i, p).start()
    meanwhile(2)
    for i in range(heads):
        attn_ref[:, i * head_dim:(i + 1) * head_dim] = cs[
            i * req_count:(i + 1) * req_count, :
        ].astype(jnp.bfloat16)
    gather_rows(0, 2 * ZN)
    for p in parts:
        for i in range(2 * ZN, 4 * ZN):
            arrived(i, p)
    gather_rows(2 * ZN, 4 * ZN)

    per_expert = hid_units * ZN * XN // EXPERTS
    first_expert = sec * (EXPERTS // (ZN * XN))


    def spread_of(shape, first, unit_dim):
        expert = lax.broadcasted_iota(jnp.int32, shape, 1 - unit_dim) % EXPERTS - first_expert
        at = lax.broadcasted_iota(jnp.int32, shape, unit_dim) + first - expert * per_expert
        return jnp.where((at >= 0) & (at < per_expert), 1.0, 0.0).astype(jnp.bfloat16)

    def project_turned(c):
        first = c * UNITS
        gate_act = jnp.dot(xs[:, 0:model_dim], flip[0, c], preferred_element_type=jnp.float32)
        up_act = jnp.dot(xs[:, 0:model_dim], flip[1, c], preferred_element_type=jnp.float32)
        share_of = jnp.dot(
            xs[:, model_dim:model_dim + GATE_LANES], spread_of((GATE_LANES, UNITS), first, 1),
            preferred_element_type=jnp.float32,
        )
        hidden = gate_act / (1.0 + jnp.exp(-gate_act)) * up_act
        hid[:, first:first + UNITS] = (hidden * share_of).astype(jnp.bfloat16)

    def project(first, count):
        rows = pl.ds(first, count)
        gate_act = lax.dot_general(
            wg[rows, :], xs[:, 0:model_dim], (((1,), (1,)), ((), ())),
            preferred_element_type=jnp.float32,
        )
        up_act = lax.dot_general(
            wu[rows, :], xs[:, 0:model_dim], (((1,), (1,)), ((), ())),
            preferred_element_type=jnp.float32,
        )
        share_of = lax.dot_general(
            spread_of((count, GATE_LANES), first, 0), xs[:, model_dim:model_dim + GATE_LANES],
            (((1,), (1,)), ((), ())), preferred_element_type=jnp.float32,
        )
        hidden = gate_act / (1.0 + jnp.exp(-gate_act)) * up_act
        hid[:, rows] = (hidden * share_of).astype(jnp.bfloat16).T

    for c in range(steps):
        for which in range(2):
            need(c, which)
    count = (hid_units - turned) // BODIES
    blocks = BESIDE * UNITS // TURN
    ready, waiting = list(range(IDLE)), list(range(IDLE, IDLE + BESIDE))
    for body in range(BODIES):
        last = blocks * (body + 1) // BODIES
        for i in range(blocks * body // BODIES, last):
            for which in range(2):
                turn(which, IDLE * UNITS // TURN + i)
        if ready:
            project_turned(ready.pop(0))
        if count:
            project(turned + body * count, count)
        while waiting and (waiting[0] - IDLE + 1) * UNITS <= last * TURN:
            ready.append(waiting.pop(0))
    for c in ready:
        project_turned(c)

    half = SLOTS * tok_rows // 2

    def send(c, stage, src, dst, peer):
        return pltpu.make_async_remote_copy(
            src_ref=src, dst_ref=dst,
            send_sem=rs_send.at[c, stage], recv_sem=rs_recv.at[c, stage],
            device_id=peer, device_id_type=MESH_ID,
        )

    def stage1(c):
        return send(c, 0, send1.at[c], recv1.at[c], h_peer)

    def stage_x(c):
        return send(c, ZN, send2.at[c, pl.ds(ZN, ZN)], recv2.at[c, pl.ds(ZN, ZN)], x_peer)

    def stage2(c):
        return [
            send(c, k, send2.at[c, k], recv2.at[c, k], far_peer(k))
            for k in range(1, ZN if c in VIA_X else ZN * XN)
        ]

    def down(c):
        wd_copy(c).wait()
        part = jnp.dot(
            hid[...], wd[:, c * COLS:(c + 1) * COLS], preferred_element_type=jnp.float32
        )
        own1[c] = part[0:half]
        send1[c] = part[half:2 * half].astype(jnp.bfloat16)
        stage1(c).start()

    def after1(c):
        stage1(c).wait_recv()
        total = own1[c] + recv1[c].astype(jnp.float32)
        if c in VIA_X:
            for k in range(ZN, ZN * XN):
                send2[c, k] = total[k * tok_rows:(k + 1) * tok_rows].astype(jnp.bfloat16)
            stage_x(c).start()
            own1[c, 0:ZN * tok_rows] = total[0:ZN * tok_rows]
        else:
            spread_out(c, total, ZN * XN)

    def spread_out(c, total, count):
        own2[c] = total[0:tok_rows]
        for k in range(1, count):
            send2[c, k] = total[k * tok_rows:(k + 1) * tok_rows].astype(jnp.bfloat16)
        for copy in stage2(c):
            copy.start()

    def after_x(c):
        stage_x(c).wait_recv()
        other = recv2[c, ZN:ZN * XN].astype(jnp.float32).reshape(ZN * tok_rows, COLS)
        spread_out(c, own1[c, 0:ZN * tok_rows] + other, ZN)

    def after2(c):
        for copy in stage2(c):
            copy.wait_recv()
        total = own2[c]
        for k in range(1, ZN if c in VIA_X else ZN * XN):
            total = total + recv2[c, k].astype(jnp.float32)
        out_ref[:, c * COLS:(c + 1) * COLS] = total.astype(jnp.bfloat16)

    for step in range(col_steps + LAG):
        if step < col_steps:
            down(step)
        if step >= LAG:
            after1(step - LAG)
    for c in VIA_X:
        after_x(c)
    for c in range(col_steps):
        if c not in VIA_X:
            after2(c)
    for c in VIA_X:
        after2(c)
    for p in parts:
        for k in range(1, ZN):
            z_share(k, p).wait_send()
        for i in range(ZN):
            x_share(i, p).wait_send()
        for i in range(ZN * XN):
            h_share(i, p).wait_send()
    for c in range(col_steps):
        for copy in [stage1(c)] + stage2(c) + ([stage_x(c)] if c in VIA_X else []):
            copy.wait_send()


def fused_device(
    queries, key_cache, value_cache, new_keys, new_values, history,
    tokens, expert_ids, gate_values, w_gate, w_up, w_down,
):
    req_count, length, kv_local, head_dim = key_cache.shape
    tok_rows, model_dim = tokens.shape
    units = w_gate.shape[0] * w_gate.shape[1]
    keys = key_cache.reshape(req_count, length * kv_local, head_dim)
    values = value_cache.reshape(req_count, length * kv_local, head_dim)
    heads = queries.shape[1] // head_dim
    rows = SLOTS * tok_rows
    wide = model_dim + GATE_LANES
    blocks = model_dim // COLS
    bf16, f32 = jnp.bfloat16, jnp.float32
    vmem = pl.BlockSpec(memory_space=pltpu.VMEM)
    hbm = pl.BlockSpec(memory_space=pltpu.HBM)
    return pl.pallas_call(
        fused_kernel,
        out_shape=(pltpu.VMEM(queries.shape, bf16), pltpu.VMEM(tokens.shape, bf16)),
        in_specs=[pl.BlockSpec(memory_space=pltpu.SMEM)] + [hbm] * 11,
        out_specs=(vmem, vmem),
        scratch_shapes=[
            pltpu.VMEM(queries.shape, bf16),
            pltpu.VMEM(new_keys.shape, bf16),
            pltpu.VMEM(new_values.shape, bf16),
            pltpu.VMEM(tokens.shape, bf16),
            pltpu.VMEM(expert_ids.shape, jnp.int32),
            pltpu.VMEM(gate_values.shape, f32),
            pltpu.VMEM(keys.shape, bf16),
            pltpu.VMEM(values.shape, bf16),
            pltpu.VMEM((units, model_dim), bf16),
            pltpu.VMEM((units, model_dim), bf16),
            pltpu.VMEM((units, model_dim), bf16),
            pltpu.VMEM((2, max(IDLE + BESIDE, 1), model_dim, UNITS), bf16),
            pltpu.VMEM((heads * req_count, head_dim), f32),
            pltpu.VMEM((heads * req_count, head_dim), f32),
            pltpu.VMEM((SLOTS, tok_rows, wide), bf16),
            pltpu.VMEM((rows, wide), bf16),
            pltpu.VMEM((rows, units), bf16),
            pltpu.VMEM((blocks, rows // 2, COLS), f32),
            pltpu.VMEM((blocks, tok_rows, COLS), f32),
            pltpu.VMEM((blocks, rows // 2, COLS), bf16),
            pltpu.VMEM((blocks, ZN * XN, tok_rows, COLS), bf16),
            pltpu.VMEM((blocks, rows // 2, COLS), bf16),
            pltpu.VMEM((blocks, ZN * XN, tok_rows, COLS), bf16),
            pltpu.SemaphoreType.DMA((6,)),
            pltpu.SemaphoreType.DMA((2, req_count)),
            pltpu.SemaphoreType.DMA((2, units // UNITS)),
            pltpu.SemaphoreType.DMA((blocks,)),
            pltpu.SemaphoreType.DMA((len(SPLITS) - 1, SLOTS)),
            pltpu.SemaphoreType.DMA((len(SPLITS) - 1, SLOTS)),
            pltpu.SemaphoreType.DMA((blocks, ZN * XN)),
            pltpu.SemaphoreType.DMA((blocks, ZN * XN)),
        ],
        compiler_params=pltpu.CompilerParams(
            collective_id=0, has_side_effects=True, vmem_limit_bytes=60 * 1024 * 1024
        ),
    )(
        history, queries, new_keys, new_values, tokens, expert_ids, gate_values,
        keys, values,
        w_gate.reshape(units, model_dim), w_up.reshape(units, model_dim),
        w_down.reshape(units, model_dim),
    )


def solution(mesh):
    in_specs = (
        P(("group", "sec"), "head"),
        P(("group", "sec"), None, "head", None),
        P(("group", "sec"), None, "head", None),
        P(("group", "sec"), "head"),
        P(("group", "sec"), "head"),
        P(("group", "sec")),
        P(("group", "sec", "head"), None),
        P(("group", "sec", "head"), None),
        P(("group", "sec", "head"), None),
        P("sec", "head", None),
        P("sec", "head", None),
        P("sec", "head", None),
    )
    out_specs = (P(("group", "sec"), "head"), P(("group", "sec", "head"), None))
    small = mesh.shape["sec"] == ZN * XN and mesh.shape["head"] == HN
    return jax.shard_map(
        fused_device if small else per_device, mesh=mesh, in_specs=in_specs, out_specs=out_specs, check_vma=False
    )
```

```python
import functools

import jax
import jax.numpy as jnp
from jax import lax
from jax.experimental import pallas as pl
from jax.experimental.pallas import tpu as pltpu
from jax.sharding import PartitionSpec as P

EXPERTS = 64
HQ = 64
KVH = 4
CAP = 2


def attention_block(queries, key_cache, value_cache, new_keys, new_values, history):
    req_count, length, kv_local, head_dim = key_cache.shape
    groups = HQ // KVH
    scaling = head_dim ** (-0.5)
    query4 = queries.reshape(req_count, kv_local, groups, head_dim)
    scores = (
        jnp.einsum("rjgd,rljd->rjgl", query4, key_cache, preferred_element_type=jnp.float32)
        * scaling
    )
    fresh_keys = new_keys.reshape(req_count, kv_local, head_dim)
    own_score = (
        jnp.einsum("rjgd,rjd->rjg", query4, fresh_keys, preferred_element_type=jnp.float32)
        * scaling
    )
    usable = jnp.arange(length, dtype=jnp.int32)[None, :] < history[:, None]
    scores = jnp.where(usable[:, None, None, :], scores, -1e30)
    peak = jnp.maximum(jnp.max(scores, axis=-1), own_score)
    exp_terms = jnp.exp(scores - peak[..., None])
    own_exp = jnp.exp(own_score - peak)
    totals = jnp.sum(exp_terms, axis=-1) + own_exp
    attn_weights = (exp_terms / totals[..., None]).astype(jnp.bfloat16)
    own_weight = (own_exp / totals).astype(jnp.bfloat16)
    mixture = jnp.einsum(
        "rjgl,rljd->rjgd", attn_weights, value_cache, preferred_element_type=jnp.float32
    )
    fresh_values = new_values.reshape(req_count, kv_local, head_dim).astype(jnp.float32)
    mixture = mixture + own_weight.astype(jnp.float32)[..., None] * fresh_values[:, :, None, :]
    return mixture.astype(jnp.bfloat16).reshape(req_count, kv_local * groups * head_dim)


def per_device(
    queries,
    key_cache,
    value_cache,
    new_keys,
    new_values,
    history,
    tokens,
    expert_ids,
    gate_values,
    w_gate,
    w_up,
    w_down,
):
    attn_context = attention_block(queries, key_cache, value_cache, new_keys, new_values, history)
    tok_rows, top_k = expert_ids.shape
    model_dim = tokens.shape[1]
    sec_count = lax.axis_size("sec")
    per_dev = w_gate.shape[0]
    flat_ids = expert_ids.reshape(-1)
    order = jnp.arange(flat_ids.shape[0], dtype=jnp.int32)
    earlier = (flat_ids[:, None] == flat_ids[None, :]) & (order[None, :] < order[:, None])
    slot_of = jnp.sum(earlier.astype(jnp.int32), axis=1)
    target = flat_ids * CAP + slot_of
    matches = (target[None, :] == jnp.arange(EXPERTS * CAP, dtype=jnp.int32)[:, None]).reshape(
        EXPERTS * CAP, tok_rows, top_k
    )
    placing = jnp.any(matches, axis=2).astype(jnp.bfloat16)
    outgoing = jnp.dot(placing, tokens, preferred_element_type=jnp.float32).astype(jnp.bfloat16)
    doubled = jnp.broadcast_to(
        outgoing.reshape(EXPERTS, 1, CAP, model_dim), (EXPERTS, 2, CAP, model_dim)
    ).reshape(sec_count, per_dev, CAP, model_dim)
    weighting = jnp.transpose(jnp.sum(jnp.where(matches, gate_values[None, :, :], 0.0), axis=2))
    both_rows = lax.all_gather(
        lax.all_to_all(doubled, "sec", split_axis=0, concat_axis=0, tiled=True),
        "head",
        axis=0,
        tiled=True,
    )
    gate_act = jnp.einsum("smcd,mfd->smcf", both_rows, w_gate, preferred_element_type=jnp.float32)
    up_act = jnp.einsum("smcd,mfd->smcf", both_rows, w_up, preferred_element_type=jnp.float32)
    hidden = (jax.nn.silu(gate_act) * up_act).astype(jnp.bfloat16)
    part_sums = jnp.einsum("smcf,mfd->smcd", hidden, w_down, preferred_element_type=jnp.float32)
    half_out = lax.psum_scatter(
        part_sums.astype(jnp.bfloat16), "head", scatter_dimension=0, tiled=True
    )
    returned = lax.all_to_all(half_out, "sec", split_axis=0, concat_axis=0, tiled=True)
    expert_sum = jnp.sum(
        returned.reshape(EXPERTS, 2, CAP, model_dim).astype(jnp.float32), axis=1
    ).reshape(EXPERTS * CAP, model_dim)
    expert_output = jnp.dot(
        weighting, expert_sum, precision=lax.Precision.HIGHEST, preferred_element_type=jnp.float32
    ).astype(jnp.bfloat16)
    return (attn_context, expert_output)


ZN, XN, HN = 4, 2, 2
SLOTS = ZN * XN * HN
UNITS = 512
COLS = 512
LAG = 1
GATE_LANES = 128
MESH_ID = pl.DeviceIdType.MESH
EARLY = 1
IDLE, BESIDE = 1, 3
BODIES = 4
TURN = 128
FILL = (4, 3, 1)
ATT = (2, 1, 1)
SPLITS = (0, 2176)
VIA_X = (0, 1)
UNROLL = False
ZORDER = (1, 2, 3)


def fused_kernel(
    hist_ref,
    q_hbm, nk_hbm, nv_hbm, tok_hbm, ids_hbm, gv_hbm,
    key_hbm, val_hbm, wg_hbm, wu_hbm, wd_hbm,
    attn_ref, out_ref,
    q_ref, nk_ref, nv_ref, tok_ref, ids_ref, gv_ref,
    kbuf, vbuf, wg, wu, wd, flip, qs, cs, xg, xs, hid,
    own1, own2, send1, send2, recv1, recv2,
    in_sem, kv_sem, gu_sem, wd_sem, ag_send, ag_recv, rs_send, rs_recv,
):
    tok_rows, model_dim = tok_ref.shape
    hid_units = wg_hbm.shape[0]
    steps = hid_units // UNITS
    col_steps = model_dim // COLS
    req_count = key_hbm.shape[0]
    heads, head_dim = q_ref.shape[1] // key_hbm.shape[2], key_hbm.shape[2]
    sec = lax.axis_index("sec")
    core = lax.axis_index("head")
    z, x = sec // XN, sec % XN
    x_peer = {"sec": z * XN + (x + 1) % XN, "head": core}
    h_peer = {"sec": sec, "head": (core + 1) % HN}

    def z_peer(k):
        return {"sec": ((z + k) % ZN) * XN + x, "head": core}

    def far_peer(k):
        return {"sec": ((z + k % ZN) % ZN) * XN + (x + k // ZN) % XN, "head": core}

    barrier = pltpu.get_barrier_semaphore()
    for peer in [far_peer(k) for k in range(1, ZN * XN)] + [h_peer]:
        pl.semaphore_signal(barrier, inc=1, device_id=peer, device_id_type=MESH_ID)

    small = [
        pltpu.make_async_copy(src, dst, in_sem.at[i])
        for i, (src, dst) in enumerate([
            (tok_hbm, tok_ref), (ids_hbm, ids_ref), (gv_hbm, gv_ref),
            (q_hbm, q_ref), (nk_hbm, nk_ref), (nv_hbm, nv_ref),
        ])
    ]

    def kv_copies(r):
        return (
            pltpu.make_async_copy(key_hbm.at[r], kbuf.at[r], kv_sem.at[0, r]),
            pltpu.make_async_copy(val_hbm.at[r], vbuf.at[r], kv_sem.at[1, r]),
        )

    def gu_copies(c):
        rows = pl.ds(pl.multiple_of(c * UNITS, UNITS), UNITS)
        return (
            pltpu.make_async_copy(wg_hbm.at[rows], wg.at[rows], gu_sem.at[0, c]),
            pltpu.make_async_copy(wu_hbm.at[rows], wu.at[rows], gu_sem.at[1, c]),
        )

    def wd_copy(c):
        cols = pl.ds(c * COLS, COLS)
        return pltpu.make_async_copy(wd_hbm.at[:, cols], wd.at[:, cols], wd_sem.at[c])

    for copy in small:
        copy.start()
    for r in range(req_count):
        for copy in kv_copies(r):
            copy.start()
    def start_weights(lo, hi):
        for c in range(lo, hi):
            for copy in gu_copies(c):
                copy.start()

    start_weights(0, EARLY)
    for copy in small[0:3]:
        copy.wait()
    lane = lax.broadcasted_iota(jnp.int32, (tok_rows, GATE_LANES), 1)
    weight = jnp.zeros((tok_rows, GATE_LANES), jnp.float32)
    ids = ids_ref[...]
    gates = gv_ref[...]
    for k in range(ids_ref.shape[1]):
        weight = weight + jnp.where(lane % EXPERTS == ids[:, k:k + 1], gates[:, k:k + 1], 0.0)
    upper = weight.astype(jnp.bfloat16).astype(jnp.float32)
    xg[0, :, 0:model_dim] = tok_ref[...]
    xg[0, :, model_dim:model_dim + GATE_LANES] = jnp.where(
        lane < EXPERTS, upper, weight - upper
    ).astype(jnp.bfloat16)

    pl.semaphore_wait(barrier, ZN * XN)

    parts = range(len(SPLITS) - 1)

    def share(src, dst, peer, p):
        cols = pl.ds(SPLITS[p], SPLITS[p + 1] - SPLITS[p])
        return pltpu.make_async_remote_copy(
            src_ref=xg.at[src, :, cols], dst_ref=xg.at[dst, :, cols],
            send_sem=ag_send.at[p, dst], recv_sem=ag_recv.at[p, dst],
            device_id=peer, device_id_type=MESH_ID,
        )

    def z_share(k, p):
        return share(0, (ZN - k) % ZN, z_peer(k), p)

    def x_share(i, p):
        return share(i, ZN + i, x_peer, p)

    def h_share(i, p):
        return share(i, ZN * XN + i, h_peer, p)

    for p in parts:
        for k in ZORDER:
            z_share(k, p).start()
        x_share(0, p).start()
    for p in parts:
        h_share(0, p).start()

    start_weights(EARLY, steps)
    for c in range(col_steps):
        wd_copy(c).start()

    per_kv = heads // 2
    for copy in small[3:6]:
        copy.wait()
    for i in range(heads):
        qs[i * req_count:(i + 1) * req_count, :] = q_ref[
            :, i * head_dim:(i + 1) * head_dim
        ].astype(jnp.float32)
    scaling = head_dim ** (-0.5)
    places = kbuf.shape[1]
    row_id = lax.broadcasted_iota(jnp.int32, (heads, places), 0)
    col_id = lax.broadcasted_iota(jnp.int32, (heads, places), 1)
    same_head = (col_id % 2) == (row_id // per_kv)
    position = col_id // 2
    low_head = lax.broadcasted_iota(jnp.int32, (heads, head_dim), 0) < per_kv

    def attend(r):
        for copy in kv_copies(r):
            copy.wait()
        query = qs[pl.ds(r, heads, stride=req_count), :]
        scores = lax.dot_general(
            query.astype(jnp.bfloat16), kbuf[r], (((1,), (1,)), ((), ())),
            preferred_element_type=jnp.float32,
        ) * scaling
        scores = jnp.where(same_head & (position < hist_ref[r]), scores, -1e30)
        nk = nk_ref[r:r + 1, :].astype(jnp.float32)
        nv = nv_ref[r:r + 1, :].astype(jnp.float32)
        fresh_key = jnp.where(low_head, nk[:, 0:head_dim], nk[:, head_dim:2 * head_dim])
        fresh_value = jnp.where(low_head, nv[:, 0:head_dim], nv[:, head_dim:2 * head_dim])
        own_score = jnp.sum(query * fresh_key, axis=1, keepdims=True) * scaling
        peak = jnp.maximum(jnp.max(scores, axis=1, keepdims=True), own_score)
        terms = jnp.exp(scores - peak)
        own_term = jnp.exp(own_score - peak)
        inverse = 1.0 / (jnp.sum(terms, axis=1, keepdims=True) + own_term)
        mixture = jnp.dot(
            (terms * inverse).astype(jnp.bfloat16), vbuf[r],
            preferred_element_type=jnp.float32,
        )
        own_weight = (own_term * inverse).astype(jnp.bfloat16).astype(jnp.float32)
        cs[pl.ds(r, heads, stride=req_count), :] = mixture + own_weight * fresh_value

    turned = (IDLE + BESIDE) * UNITS
    arrived_units = set()

    def need(c, which):
        if (c, which) not in arrived_units:
            arrived_units.add((c, which))
            gu_copies(c)[which].wait()

    def turn(which, i):
        need(i * TURN // UNITS, which)
        first = i * TURN
        source = (wg, wu)[which]
        flip[which, first // UNITS, :, first % UNITS:first % UNITS + TURN] = source[first:first + TURN, :].T

    jobs = [(w, i) for i in range(IDLE * UNITS // TURN) for w in range(2)]
    seats = list(range(req_count))

    def meanwhile(place):
        for _ in range(ATT[place]):
            attend(seats.pop(0))
        for _ in range(FILL[place]):
            if jobs:
                turn(*jobs.pop(0))

    def arrived(i, p):
        share(i, i, x_peer, p).wait_recv()

    def gather_rows(lo, hi):
        rows = xg[lo:hi].astype(jnp.float32).reshape((hi - lo) * tok_rows, xg.shape[2])
        xs[lo * tok_rows:hi * tok_rows, :] = rows.astype(jnp.bfloat16)

    meanwhile(0)
    for p in parts:
        for i in range(1, ZN):
            arrived(i, p)
            x_share(i, p).start()
            h_share(i, p).start()
    for p in parts:
        arrived(ZN, p)
        h_share(ZN, p).start()
    meanwhile(1)
    for p in parts:
        for i in range(ZN + 1, 2 * ZN):
            arrived(i, p)
            h_share(i, p).start()
    meanwhile(2)
    for i in range(heads):
        attn_ref[:, i * head_dim:(i + 1) * head_dim] = cs[
            i * req_count:(i + 1) * req_count, :
        ].astype(jnp.bfloat16)
    gather_rows(0, 2 * ZN)
    for p in parts:
        for i in range(2 * ZN, 4 * ZN):
            arrived(i, p)
    gather_rows(2 * ZN, 4 * ZN)

    per_expert = hid_units * ZN * XN // EXPERTS
    first_expert = sec * (EXPERTS // (ZN * XN))


    def spread_of(shape, first, unit_dim):
        expert = lax.broadcasted_iota(jnp.int32, shape, 1 - unit_dim) % EXPERTS - first_expert
        at = lax.broadcasted_iota(jnp.int32, shape, unit_dim) + first - expert * per_expert
        return jnp.where((at >= 0) & (at < per_expert), 1.0, 0.0).astype(jnp.bfloat16)

    def project_turned(c):
        first = c * UNITS
        gate_act = jnp.dot(xs[:, 0:model_dim], flip[0, c], preferred_element_type=jnp.float32)
        up_act = jnp.dot(xs[:, 0:model_dim], flip[1, c], preferred_element_type=jnp.float32)
        share_of = jnp.dot(
            xs[:, model_dim:model_dim + GATE_LANES], spread_of((GATE_LANES, UNITS), first, 1),
            preferred_element_type=jnp.float32,
        )
        hidden = gate_act / (1.0 + jnp.exp(-gate_act)) * up_act
        hid[:, first:first + UNITS] = (hidden * share_of).astype(jnp.bfloat16)

    def project(first, count):
        rows = pl.ds(first, count)
        gate_act = lax.dot_general(
            wg[rows, :], xs[:, 0:model_dim], (((1,), (1,)), ((), ())),
            preferred_element_type=jnp.float32,
        )
        up_act = lax.dot_general(
            wu[rows, :], xs[:, 0:model_dim], (((1,), (1,)), ((), ())),
            preferred_element_type=jnp.float32,
        )
        share_of = lax.dot_general(
            spread_of((count, GATE_LANES), first, 0), xs[:, model_dim:model_dim + GATE_LANES],
            (((1,), (1,)), ((), ())), preferred_element_type=jnp.float32,
        )
        hidden = gate_act / (1.0 + jnp.exp(-gate_act)) * up_act
        hid[:, rows] = (hidden * share_of).astype(jnp.bfloat16).T

    for c in range(steps):
        for which in range(2):
            need(c, which)
    count = (hid_units - turned) // BODIES
    blocks = BESIDE * UNITS // TURN
    ready, waiting = list(range(IDLE)), list(range(IDLE, IDLE + BESIDE))
    for body in range(BODIES):
        last = blocks * (body + 1) // BODIES
        for i in range(blocks * body // BODIES, last):
            for which in range(2):
                turn(which, IDLE * UNITS // TURN + i)
        if ready:
            project_turned(ready.pop(0))
        if count:
            project(turned + body * count, count)
        while waiting and (waiting[0] - IDLE + 1) * UNITS <= last * TURN:
            ready.append(waiting.pop(0))
    for c in ready:
        project_turned(c)

    half = SLOTS * tok_rows // 2

    def send(c, stage, src, dst, peer):
        return pltpu.make_async_remote_copy(
            src_ref=src, dst_ref=dst,
            send_sem=rs_send.at[c, stage], recv_sem=rs_recv.at[c, stage],
            device_id=peer, device_id_type=MESH_ID,
        )

    def stage1(c):
        return send(c, 0, send1.at[c], recv1.at[c], h_peer)

    def stage_x(c):
        return send(c, ZN, send2.at[c, pl.ds(ZN, ZN)], recv2.at[c, pl.ds(ZN, ZN)], x_peer)

    def stage2(c):
        return [
            send(c, k, send2.at[c, k], recv2.at[c, k], far_peer(k))
            for k in range(1, ZN if c in VIA_X else ZN * XN)
        ]

    def down(c):
        wd_copy(c).wait()
        part = jnp.dot(
            hid[...], wd[:, c * COLS:(c + 1) * COLS], preferred_element_type=jnp.float32
        )
        own1[c] = part[0:half]
        send1[c] = part[half:2 * half].astype(jnp.bfloat16)
        stage1(c).start()

    def after1(c):
        stage1(c).wait_recv()
        total = own1[c] + recv1[c].astype(jnp.float32)
        if c in VIA_X:
            for k in range(ZN, ZN * XN):
                send2[c, k] = total[k * tok_rows:(k + 1) * tok_rows].astype(jnp.bfloat16)
            stage_x(c).start()
            own1[c, 0:ZN * tok_rows] = total[0:ZN * tok_rows]
        else:
            spread_out(c, total, ZN * XN)

    def spread_out(c, total, count):
        own2[c] = total[0:tok_rows]
        for k in range(1, count):
            send2[c, k] = total[k * tok_rows:(k + 1) * tok_rows].astype(jnp.bfloat16)
        for copy in stage2(c):
            copy.start()

    def after_x(c):
        stage_x(c).wait_recv()
        other = recv2[c, ZN:ZN * XN].astype(jnp.float32).reshape(ZN * tok_rows, COLS)
        spread_out(c, own1[c, 0:ZN * tok_rows] + other, ZN)

    def after2(c):
        for copy in stage2(c):
            copy.wait_recv()
        total = own2[c]
        for k in range(1, ZN if c in VIA_X else ZN * XN):
            total = total + recv2[c, k].astype(jnp.float32)
        out_ref[:, c * COLS:(c + 1) * COLS] = total.astype(jnp.bfloat16)

    for step in range(col_steps + LAG):
        if step < col_steps:
            down(step)
        if step >= LAG:
            after1(step - LAG)
    for c in VIA_X:
        after_x(c)
    for c in range(col_steps):
        if c not in VIA_X:
            after2(c)
    for c in VIA_X:
        after2(c)
    for p in parts:
        for k in range(1, ZN):
            z_share(k, p).wait_send()
        for i in range(ZN):
            x_share(i, p).wait_send()
        for i in range(ZN * XN):
            h_share(i, p).wait_send()
    for c in range(col_steps):
        for copy in [stage1(c)] + stage2(c) + ([stage_x(c)] if c in VIA_X else []):
            copy.wait_send()


def fused_device(
    queries, key_cache, value_cache, new_keys, new_values, history,
    tokens, expert_ids, gate_values, w_gate, w_up, w_down,
):
    req_count, length, kv_local, head_dim = key_cache.shape
    tok_rows, model_dim = tokens.shape
    units = w_gate.shape[0] * w_gate.shape[1]
    keys = key_cache.reshape(req_count, length * kv_local, head_dim)
    values = value_cache.reshape(req_count, length * kv_local, head_dim)
    heads = queries.shape[1] // head_dim
    rows = SLOTS * tok_rows
    wide = model_dim + GATE_LANES
    blocks = model_dim // COLS
    bf16, f32 = jnp.bfloat16, jnp.float32
    vmem = pl.BlockSpec(memory_space=pltpu.VMEM)
    hbm = pl.BlockSpec(memory_space=pltpu.HBM)
    return pl.pallas_call(
        fused_kernel,
        out_shape=(pltpu.VMEM(queries.shape, bf16), pltpu.VMEM(tokens.shape, bf16)),
        in_specs=[pl.BlockSpec(memory_space=pltpu.SMEM)] + [hbm] * 11,
        out_specs=(vmem, vmem),
        scratch_shapes=[
            pltpu.VMEM(queries.shape, bf16),
            pltpu.VMEM(new_keys.shape, bf16),
            pltpu.VMEM(new_values.shape, bf16),
            pltpu.VMEM(tokens.shape, bf16),
            pltpu.VMEM(expert_ids.shape, jnp.int32),
            pltpu.VMEM(gate_values.shape, f32),
            pltpu.VMEM(keys.shape, bf16),
            pltpu.VMEM(values.shape, bf16),
            pltpu.VMEM((units, model_dim), bf16),
            pltpu.VMEM((units, model_dim), bf16),
            pltpu.VMEM((units, model_dim), bf16),
            pltpu.VMEM((2, max(IDLE + BESIDE, 1), model_dim, UNITS), bf16),
            pltpu.VMEM((heads * req_count, head_dim), f32),
            pltpu.VMEM((heads * req_count, head_dim), f32),
            pltpu.VMEM((SLOTS, tok_rows, wide), bf16),
            pltpu.VMEM((rows, wide), bf16),
            pltpu.VMEM((rows, units), bf16),
            pltpu.VMEM((blocks, rows // 2, COLS), f32),
            pltpu.VMEM((blocks, tok_rows, COLS), f32),
            pltpu.VMEM((blocks, rows // 2, COLS), bf16),
            pltpu.VMEM((blocks, ZN * XN, tok_rows, COLS), bf16),
            pltpu.VMEM((blocks, rows // 2, COLS), bf16),
            pltpu.VMEM((blocks, ZN * XN, tok_rows, COLS), bf16),
            pltpu.SemaphoreType.DMA((6,)),
            pltpu.SemaphoreType.DMA((2, req_count)),
            pltpu.SemaphoreType.DMA((2, units // UNITS)),
            pltpu.SemaphoreType.DMA((blocks,)),
            pltpu.SemaphoreType.DMA((len(SPLITS) - 1, SLOTS)),
            pltpu.SemaphoreType.DMA((len(SPLITS) - 1, SLOTS)),
            pltpu.SemaphoreType.DMA((blocks, ZN * XN)),
            pltpu.SemaphoreType.DMA((blocks, ZN * XN)),
        ],
        compiler_params=pltpu.CompilerParams(
            collective_id=0, has_side_effects=True, vmem_limit_bytes=60 * 1024 * 1024
        ),
    )(
        history, queries, new_keys, new_values, tokens, expert_ids, gate_values,
        keys, values,
        w_gate.reshape(units, model_dim), w_up.reshape(units, model_dim),
        w_down.reshape(units, model_dim),
    )


def solution(mesh):
    in_specs = (
        P(("group", "sec"), "head"),
        P(("group", "sec"), None, "head", None),
        P(("group", "sec"), None, "head", None),
        P(("group", "sec"), "head"),
        P(("group", "sec"), "head"),
        P(("group", "sec")),
        P(("group", "sec", "head"), None),
        P(("group", "sec", "head"), None),
        P(("group", "sec", "head"), None),
        P("sec", "head", None),
        P("sec", "head", None),
        P("sec", "head", None),
    )
    out_specs = (P(("group", "sec"), "head"), P(("group", "sec", "head"), None))
    small = mesh.shape["sec"] == ZN * XN and mesh.shape["head"] == HN
    return jax.shard_map(
        fused_device if small else per_device, mesh=mesh, in_specs=in_specs, out_specs=out_specs, check_vma=False
    )
```
